512 devices in a mesh: cfg: 2 (over core), seq: 64 (over x, z, y_hi), tp: 4 (over y_lo).
Axes of the slice: x: 4, y: 8 (y_hi: 2, y_lo: 4; y = y_hi * 4 + y_lo), z: 8, core: 2. Of those that a mesh axis runs over, the one named last changes fastest.
Arguments:
- stream: bfloat16 [2, 2560, 3072], P('cfg', 'seq', 'tp'), may hold values from -6 to 6
- queries: bfloat16 [2, 2560, 1536], P('cfg', 'seq', 'tp'), may hold values from -6 to 6
- keys: bfloat16 [2, 2560, 1536], P('cfg', 'seq', 'tp'), may hold values from -6 to 6
- values: bfloat16 [2, 2560, 1536], P('cfg', 'seq', 'tp'), may hold values from -6 to 6
- text_keys: bfloat16 [2, 226, 1536], P('cfg', None, 'tp'), may hold values from -6 to 6
- text_values: bfloat16 [2, 226, 1536], P('cfg', None, 'tp'), may hold values from -6 to 6
- out_weight: bfloat16 [1536, 3072], P('tp'), may hold values from -0.15625 to 0.15625
- gate: float32 [3072], P('tp'), may hold values from -4 to 4
- shift: float32 [3072], P('tp'), may hold values from -3 to 3
- scale: float32 [3072], P('tp'), may hold values from -3 to 3
- proj_weight: float32 [3072, 64], P('tp'), may hold values from -0.109375 to 0.109375
- q_gain: float32 [64], replicated, may hold values from 1.4 to 6
- k_gain: float32 [64], replicated, may hold values from 1.4 to 6
- lengths: int32 [64], replicated, may hold values from 1 to 40, 2304 in all
- latents: float32 [2560, 64], P('seq', ('cfg', 'tp')), may hold values from -6 to 6
- alphas: float32 [1000], replicated, may hold values from 0.05 to 0.95
- step_index: int32 [1], replicated, may hold values from 20 to 999
Outputs:
- hidden_out: bfloat16 [2, 2560, 3072], P('cfg', 'seq', 'tp')
- latents_out: float32 [2560, 64], P('seq', ('cfg', 'tp'))
The draws below stay inside these ranges and needn't reach their ends.
Inputs may be any that keep to these rules, and one draw needn't show every extreme that they name: `lengths`: video tokens held by each index of seq, in token order; they sum to 2304 and the largest is exactly 40. The previous step's entry is step_index - 20.
All inputs are finite; a program needn't handle non-finite values.
Results may differ from the reference program's by a relative error of at most 0.012.
The reference program's roundings to bfloat16 on the way (of `query_hat`, `key_hat`, `rounded` and `attended`) count: a program that leaves them out, or rounds other values in their place, can miss the bound.
Values may be sent and summed in bfloat16 or wider, within the bound.
A program may use at most 64 MiB of HBM per device.

```python
import math
import jax
import jax.numpy as jnp
import numpy as np
from jax import lax

D = 3072
HEADS = 24
HEAD = 64
TXT = 226
HP = 30
WP = 45
CHAN = 64
CAP = 40
TABLE = 1000
STRIDE = 20
HALVES = 2
ROWS = 2560
VID = 2304
N_SEQ = 64


def shared_rows(key):
    shape = (HALVES, ROWS, HEADS * HEAD)
    first = jax.random.normal(jax.random.fold_in(key, 11), shape, jnp.float32)
    second = jax.random.normal(jax.random.fold_in(key, 12), shape, jnp.float32)
    return (first, second)


def draw_queries(key, part):
    first, second = shared_rows(key)
    return jnp.clip(first, -6.0, 6.0).astype(jnp.bfloat16)


def draw_keys(key, part):
    first, second = shared_rows(key)
    return jnp.clip(second, -6.0, 6.0).astype(jnp.bfloat16)


def draw_q_gain(key, part):
    inner = jax.random.fold_in(key, 21)
    return jax.random.uniform(inner, (HEAD,), jnp.float32, 1.4, 2.4)


def draw_k_gain(key, part):
    inner = jax.random.fold_in(key, 22)
    return jax.random.uniform(inner, (HEAD,), jnp.float32, 1.4, 2.4)


def level_of(own_key, dims, cuts, low, top_value):
    def one(dim, parts):
        steps = jax.random.uniform(jax.random.fold_in(jax.random.fold_in(own_key, 6), dim), (parts,), jnp.float32, low / len(cuts), top_value / len(cuts))
        return jnp.repeat(jnp.exp(steps), dims[dim] // parts).reshape((-1,) + (1,) * (len(dims) - dim - 1))

    loudness = one(*cuts[0])
    for cut in cuts[1:]:
        loudness = loudness * one(*cut)
    return loudness


def profile(number_of, total, bound, skew):
    portions = [(1 << 20) // math.isqrt(standing ** skew) + 1 for standing in range(2, number_of + 1)]
    rest, holding = total - bound - (number_of - 1), [1] * (number_of - 1)
    while rest > 0:
        movable = [i for i in range(number_of - 1) if holding[i] < bound]
        mass, remaining = sum([portions[i] for i in movable]), rest
        for i in movable:
            extra = min(bound - holding[i], max(1, remaining * portions[i] // mass), rest)
            holding[i] = holding[i] + extra
            rest = rest - extra
    return np.array([bound] + holding)


def ragged_sizes(stream_key, count, total, limit, slope):
    if count == 2:
        one = jax.random.randint(stream_key, (), max(1, total - limit), min(limit, total - 1) + 1)
        return jnp.stack([one, total - one])
    sizes = jnp.asarray(profile(count, total, limit, slope), jnp.int32)
    couples = (count - 1) // 2
    source_of, taker = sizes[1:1 + 2 * couples:2], sizes[2:2 + 2 * couples:2]
    slack = jnp.minimum(source_of - 1, limit - taker)
    passed = jax.random.randint(jax.random.fold_in(stream_key, 1), (couples,), 0, 1 << 20) % (slack + 1)
    sizes = sizes.at[1:1 + 2 * couples:2].set(source_of - passed).at[2:2 + 2 * couples:2].set(taker + passed)
    return sizes[jax.random.permutation(jax.random.fold_in(stream_key, 2), count)]


def scatter_about(stream_key, shape, scale, reach, shards=(), held_as=jnp.bfloat16):
    entries = scale * jax.random.normal(stream_key, shape, jnp.float32)
    if shards:
        entries = entries * level_of(stream_key, shape, shards, -0.22, 0.18)
    return jnp.clip(entries, -reach, reach).astype(held_as)


def setup_inputs(seed: int = 0) -> dict:
    key_of = jax.random.split(jax.random.key(seed), 18)
    stream = scatter_about(key_of[0], (HALVES, ROWS, D), 1.0, 6.0, ((0, 2), (1, 64), (2, 4)))
    queries = draw_queries(jax.random.fold_in(key_of[17], 71), 0)
    keys = draw_keys(jax.random.fold_in(key_of[17], 71), 0)
    values = scatter_about(key_of[3], (HALVES, ROWS, HEADS * HEAD), 1.0, 6.0, ((0, 2), (1, 64), (2, 4)))
    text_keys = scatter_about(key_of[4], (HALVES, TXT, HEADS * HEAD), 1.0, 6.0, ((0, 2), (2, 4)))
    text_values = scatter_about(key_of[5], (HALVES, TXT, HEADS * HEAD), 1.0, 6.0, ((0, 2), (2, 4)))
    out_weight = scatter_about(key_of[6], (HEADS * HEAD, D), (HEADS * HEAD) ** -0.5, 0.15625, ((0, 4),))
    gate = scatter_about(key_of[7], (D,), 1.0, 4.0, ((0, 4),), jnp.float32)
    shift = scatter_about(key_of[8], (D,), 0.5, 3.0, ((0, 4),), jnp.float32)
    scale = scatter_about(key_of[9], (D,), 0.5, 3.0, ((0, 4),), jnp.float32)
    proj_weight = scatter_about(key_of[10], (D, CHAN), D ** -0.5, 0.109375, ((0, 4),), jnp.float32)
    q_gain = draw_q_gain(jax.random.fold_in(key_of[17], 71), 0)
    k_gain = draw_k_gain(jax.random.fold_in(key_of[17], 71), 0)
    lengths = ragged_sizes(key_of[13], N_SEQ, VID, CAP, 2).astype(jnp.int32)
    latents = scatter_about(key_of[14], (ROWS, CHAN), 1.0, 6.0, ((0, 64), (1, 8)), jnp.float32)
    alphas = jnp.clip(jax.random.uniform(key_of[15], (TABLE,), jnp.float32, 0.05, 0.95), 0.05, 0.95)
    step_index = jax.random.randint(key_of[16], (1,), STRIDE, TABLE).astype(jnp.int32)
    return {"stream": stream, "queries": queries, "keys": keys, "values": values, "text_keys": text_keys, "text_values": text_values, "out_weight": out_weight, "gate": gate, "shift": shift, "scale": scale, "proj_weight": proj_weight, "q_gain": q_gain, "k_gain": k_gain, "lengths": lengths, "latents": latents, "alphas": alphas, "step_index": step_index}


guide_scale = 6.0
head_eps = 1e-06
final_eps = 1e-05

def rope_tables(position):
    frame = position // (HP * WP)
    height = position // WP % HP
    across = position % WP

    def angles(coord, extent):
        freq = 1.0 / 10000.0 ** (jnp.arange(0, extent, 2, dtype=jnp.float32) / extent)
        return coord.astype(jnp.float32)[:, None] * freq[None, :]
    angle = jnp.concatenate([angles(frame, 16), angles(height, 24), angles(across, 24)], axis=1)
    return (jnp.cos(angle), jnp.sin(angle))

def head_norm(field, gain):
    centre = field - lax.optimization_barrier(jnp.mean(field, axis=-1, keepdims=True))
    spread = lax.optimization_barrier(jnp.mean(centre * centre, axis=-1, keepdims=True))
    return centre * lax.rsqrt(spread + head_eps) * gain

def rotate_pairs(field, cos_table, sin_table):
    pairs = field.reshape(field.shape[:-1] + (HEAD // 2, 2))
    first = pairs[..., 0]
    second = pairs[..., 1]
    cos_part = cos_table[:, None, :]
    sin_part = sin_table[:, None, :]
    turned = jnp.stack([first * cos_part - second * sin_part, second * cos_part + first * sin_part], axis=-1)
    return turned.reshape(field.shape)

def prepare(field, gain, tables):
    count = field.shape[0]
    normed = head_norm(field.astype(jnp.float32).reshape(count, -1, HEAD), gain)
    if tables is not None:
        normed = rotate_pairs(normed, tables[0], tables[1])
    return normed.reshape(count, -1).astype(jnp.bfloat16)

def reference(stream, queries, keys, values, text_keys, text_values, out_weight, gate, shift, scale, proj_weight, q_gain, k_gain, lengths, latents, alphas, step_index):
    offsets = jnp.cumsum(lengths) - lengths
    slots = jnp.arange(ROWS, dtype=jnp.int32)
    owner = (slots // CAP).astype(jnp.int32)
    within = (slots % CAP).astype(jnp.int32)
    position = (offsets[owner] + within).astype(jnp.int32)
    live = within < lengths[owner]
    tables = rope_tables(position)
    key_live = jnp.concatenate([jnp.arange(TXT, dtype=jnp.int32) >= 0, live])
    predictions = []
    hiddens = []
    for half in range(HALVES):
        query_hat = lax.optimization_barrier(prepare(queries[half], q_gain, tables))
        query_hat = query_hat.astype(jnp.float32).reshape(N_SEQ, CAP, HEADS, HEAD)
        key_hat = jnp.concatenate([prepare(text_keys[half], k_gain, None), prepare(keys[half], k_gain, tables)], axis=0)
        key_hat = lax.optimization_barrier(key_hat).astype(jnp.float32).reshape(-1, HEADS, HEAD)
        value_all = jnp.concatenate([text_values[half], values[half]], axis=0).astype(jnp.float32).reshape(-1, HEADS, HEAD)

        def attend(block):
            scores = jnp.einsum('qhd,khd->hqk', block, key_hat) * 0.125
            scores = jnp.where(key_live[None, None, :], scores, -jnp.inf)
            row_max = lax.optimization_barrier(jnp.max(scores, axis=-1, keepdims=True))
            weights = jnp.exp(scores - row_max)
            totals = lax.optimization_barrier(jnp.sum(weights, axis=-1))
            rounded = lax.optimization_barrier(weights.astype(jnp.bfloat16)).astype(jnp.float32)
            mixed = jnp.einsum('hqk,khd->qhd', rounded, value_all) / jnp.transpose(totals)[:, :, None]
            return mixed.astype(jnp.bfloat16).reshape(CAP, HEADS * HEAD)
        attended = lax.map(attend, query_hat).reshape(ROWS, HEADS * HEAD)
        projected = jnp.dot(attended, out_weight, preferred_element_type=jnp.float32)
        hidden = stream[half].astype(jnp.float32) + gate * projected
        hidden = jnp.where(live[:, None], hidden, 0.0).astype(jnp.bfloat16)
        hiddens.append(hidden)
        widened = lax.optimization_barrier(hidden).astype(jnp.float32)
        mean = lax.optimization_barrier(jnp.sum(widened, axis=1, keepdims=True)) / D
        square = lax.optimization_barrier(jnp.sum(widened * widened, axis=1, keepdims=True)) / D
        normed = (widened - mean) * lax.rsqrt(square - mean * mean + final_eps) * (1.0 + scale) + shift
        predictions.append(jnp.dot(normed, proj_weight, precision=lax.Precision.HIGHEST, preferred_element_type=jnp.float32))
    guided = predictions[1] + guide_scale * (predictions[0] - predictions[1])
    current = alphas[step_index[0]]
    earlier = alphas[step_index[0] - STRIDE]
    root_now = jnp.sqrt(current)
    rest_now = jnp.sqrt(1.0 - current)
    clean = root_now * latents - rest_now * guided
    noise = root_now * guided + rest_now * latents
    stepped = jnp.sqrt(earlier) * clean + jnp.sqrt(1.0 - earlier) * noise
    latents_out = jnp.where(live[:, None], stepped, 0.0)
    return (jnp.stack(hiddens), latents_out)
```

```python
import functools

import jax
import jax.numpy as jnp
import numpy as np
from jax import lax
from jax.experimental import pallas as pl
from jax.experimental.pallas import tpu as pltpu
from jax.sharding import PartitionSpec as P

NX = 4
NZ = 8
NY = 2
D = 3072
HEAD = 64
HP = 30
WP = 45
STRIDE = 20
ROWS = 40
TXT = 226
LANES = 128
PAIR = 2 * HEAD
PIECE = 8
STATS = 16

guide_scale = 6.0
head_eps = 1e-06
final_eps = 1e-05
LOW = -1e30
MESH = pl.DeviceIdType.MESH
F32 = jnp.float32
BF16 = jnp.bfloat16


def frequencies():
    def one(extent):
        return 1.0 / 10000.0 ** (np.arange(0, extent, 2, dtype=np.float32) / np.float32(extent))

    freq = np.concatenate([one(16), one(24), one(24)]).astype(np.float32)
    return np.repeat(freq, 2)[None, :].repeat(2, axis=0).reshape(1, PAIR)


def nt(left, right, precision=None):
    return lax.dot_general(
        left, right, (((1,), (1,)), ((), ())), precision=precision, preferred_element_type=F32
    )


def nn(left, right, precision=None):
    return lax.dot_general(
        left, right, (((1,), (0,)), ((), ())), precision=precision, preferred_element_type=F32
    )


def kernel(
    group,
    lengths,
    step_index,
    alphas,
    freq,
    q_gain,
    k_gain,
    stream_hbm,
    queries_hbm,
    keys_hbm,
    values_hbm,
    text_keys_hbm,
    text_values_hbm,
    weight_hbm,
    gate_hbm,
    shift_hbm,
    scale_hbm,
    proj_hbm,
    latents_hbm,
    hidden_out,
    latents_out,
    queries,
    keys,
    stream,
    text_keys,
    text_values,
    weight,
    gate,
    shift,
    scale,
    proj,
    latents,
    qbuf,
    kbuf,
    vbuf,
    osend,
    obuf,
    ssend,
    sbuf,
    rsend,
    rbuf,
    fsend,
    fbuf,
    load_sem,
    q_send,
    q_recv,
    k_send,
    k_recv,
    v_send,
    v_recv,
    o_send,
    o_recv,
    s_send,
    s_recv,
    r_send,
    r_recv,
    f_send,
    f_recv,
):
    n_kv = NX * NY
    total = 2 * group
    width = queries.shape[1]
    pairs = width // PAIR
    part = width * 2
    c = lax.axis_index("cfg")
    s = lax.axis_index("seq")
    t = lax.axis_index("tp")
    y = lax.rem(s, NY)
    z = lax.rem(lax.div(s, NY), NZ)
    x = lax.div(s, NY * NZ)
    rank = c * group + t

    def place(xx, zz, yy):
        return (c, (xx * NZ + zz) * NY + yy, t)

    z_of = [lax.rem(z + d, NZ) for d in range(1, NZ)]
    z_peers = [place(x, zz, y) for zz in z_of]
    x_of = [lax.rem(x + d, NX) for d in range(1, NX)]
    x_peers = [place(xx, z, y) for xx in x_of]
    y_peer = place(x, z, 1 - y)
    t_of = [lax.rem(t + d, group) for d in range(1, group)]
    t_peers = [(c, s, tt) for tt in t_of]
    g_of = [lax.rem(rank + d, total) for d in range(1, total)]
    g_peers = [(lax.div(g, group), s, lax.rem(g, group)) for g in g_of]

    barrier = pltpu.get_barrier_semaphore()
    everyone = z_peers + x_peers + ([y_peer] if NY > 1 else []) + g_peers
    for peer in everyone:
        pl.semaphore_signal(barrier, inc=1, device_id=peer, device_id_type=MESH)

    own = x * NY + y
    other = x * NY + (1 - y)

    loads = []

    def load(src, dst):
        copy = pltpu.make_async_copy(src, dst, load_sem.at[len(loads)])
        copy.start()
        loads.append(copy)
        return copy

    load_k = load(keys_hbm.at[0], keys)
    load_q = load(queries_hbm.at[0], queries)
    load_v = load(values_hbm.at[0], vbuf.at[own])
    load_tk = load(text_keys_hbm.at[0], text_keys)
    load_tv = load(text_values_hbm.at[0], text_values)
    load_w = [load(weight_hbm.at[:, pl.ds(j * part, part)], weight.at[j]) for j in range(group)]
    load_rest = [
        load(stream_hbm.at[0], stream),
        load(gate_hbm, gate),
        load(shift_hbm, shift),
        load(scale_hbm, scale),
        load(proj_hbm, proj),
        load(latents_hbm, latents),
    ]

    lane = lax.broadcasted_iota(jnp.int32, (1, PAIR), 1)
    within_head = lax.rem(lane, HEAD)
    is_even = lax.rem(lane, 2) == 0
    first_head = lane < HEAD
    own_start = jnp.int32(0)
    for b in range(NX * NZ * NY):
        own_start = own_start + jnp.where(b < s, lengths[b], 0)
    own_count = lengths[s]
    row = lax.broadcasted_iota(jnp.int32, (ROWS, PAIR), 0)
    live_rows = row < own_count
    position = (row + own_start).astype(F32)
    frame = jnp.floor((position + 0.5) * (1.0 / (HP * WP)))
    line = jnp.floor((position + 0.5) * (1.0 / WP))
    across = position - line * WP
    height = line - frame * HP
    coord = jnp.where(within_head < 16, frame, jnp.where(within_head < 40, height, across))
    angle = coord * freq[...]
    cos_table = jnp.cos(angle)
    sin_table = jnp.sin(angle)
    sin_table = jnp.where(is_even, -sin_table, sin_table)

    r_io = lax.broadcasted_iota(jnp.int32, (PAIR, PAIR), 0)
    c_io = lax.broadcasted_iota(jnp.int32, (PAIR, PAIR), 1)
    mean_matrix = jnp.where((r_io < HEAD) == (c_io < HEAD), 1.0 / HEAD, 0.0)
    mean_matrix_low = mean_matrix.astype(BF16)
    gain_q = jnp.concatenate([q_gain[...], q_gain[...]], axis=1)
    gain_k = jnp.concatenate([k_gain[...], k_gain[...]], axis=1)

    def head_norm(field, gain):
        centre = field.astype(F32) - nn(field, mean_matrix_low)
        spread = nn(centre * centre, mean_matrix, lax.Precision.HIGHEST)
        return centre * lax.rsqrt(spread + head_eps) * gain

    def rotate(field):
        swapped = jnp.where(
            is_even, pltpu.roll(field, PAIR - 1, 1), pltpu.roll(field, 1, 1)
        )
        return field * cos_table + swapped * sin_table

    def pair_slice(p):
        return pl.ds(p * PAIR, PAIR)

    load_k.wait()
    for p in range(pairs):
        made = rotate(head_norm(keys[:, pair_slice(p)], gain_k)).astype(BF16)
        kbuf[own, :, pair_slice(p)] = made
    load_q.wait()
    for p in range(pairs):
        made = rotate(head_norm(queries[:, pair_slice(p)], gain_q)).astype(BF16)
        qbuf[z, :, pair_slice(p)] = made

    pl.semaphore_wait(barrier, len(everyone))

    sent = []

    def send(src, dst, send_sem, recv_sem, peer):
        copy = pltpu.make_async_remote_copy(
            src_ref=src,
            dst_ref=dst,
            send_sem=send_sem,
            recv_sem=recv_sem,
            device_id=peer,
            device_id_type=MESH,
        )
        copy.start()
        sent.append(copy)

    def arrive(ref, send_sem, recv_sem, peer):
        pltpu.make_async_remote_copy(
            src_ref=ref,
            dst_ref=ref,
            send_sem=send_sem,
            recv_sem=recv_sem,
            device_id=peer,
            device_id_type=MESH,
        ).wait_recv()

    if NY > 1:
        send(values_hbm.at[0], vbuf.at[own], v_send.at[0], v_recv.at[own], y_peer)
        send(kbuf.at[own], kbuf.at[own], k_send.at[0], k_recv.at[own], y_peer)
    order_z = sorted(range(1, NZ), key=lambda d: -min(d, NZ - d))
    for d in order_z:
        send(qbuf.at[z], qbuf.at[z], q_send.at[d], q_recv.at[z], z_peers[d - 1])
    for d in range(1, NX):
        send(values_hbm.at[0], vbuf.at[own], v_send.at[d], v_recv.at[own], x_peers[d - 1])
        send(kbuf.at[own], kbuf.at[own], k_send.at[d], k_recv.at[own], x_peers[d - 1])

    load_tk.wait()
    load_tv.wait()
    text_mixed = []
    lane_row = lax.broadcasted_iota(jnp.int32, (ROWS, LANES), 1)
    text_stat = jnp.where(lax.rem(lane_row, 8) >= 6, 1.0, 0.0)
    for p in range(pairs):
        made = head_norm(text_keys[:, pair_slice(p)], gain_k)
        query_part = qbuf[z, :, pair_slice(p)]
        value_part = text_values[:, pair_slice(p)]
        outs = []
        for which in range(2):
            chosen = first_head if which == 0 else jnp.logical_not(first_head)
            key_part = jnp.where(chosen, made, 0.0).astype(BF16)
            scores = nt(query_part, key_part) * 0.125
            top = jnp.max(scores, axis=1, keepdims=True)
            weights = jnp.exp(scores - top)
            count = jnp.sum(weights, axis=1, keepdims=True)
            outs.append(nn(weights.astype(BF16), value_part))
            head = 2 * p + which
            text_stat = jnp.where(lane_row == head, top, text_stat)
            text_stat = jnp.where(lane_row == 8 + head, count, text_stat)
        text_mixed.append(jnp.where(first_head, outs[0], outs[1]))
    below = jnp.zeros((LANES - ROWS, LANES), F32)
    text_stat = jnp.concatenate([text_stat, below], axis=0).T[0:STATS]

    if NY > 1:
        arrive(vbuf.at[other], v_send.at[0], v_recv.at[other], y_peer)
        for d in range(1, NX):
            send(vbuf.at[other], vbuf.at[other], v_send.at[NX - 1 + d], v_recv.at[other], x_peers[d - 1])
        arrive(kbuf.at[other], k_send.at[0], k_recv.at[other], y_peer)
        for d in range(1, NX):
            send(kbuf.at[other], kbuf.at[other], k_send.at[NX - 1 + d], k_recv.at[other], x_peers[d - 1])
    for d in range(1, NZ):
        zz = z_of[d - 1]
        arrive(qbuf.at[zz], q_send.at[d], q_recv.at[zz], z_peers[d - 1])
    load_v.wait()
    for yy in [y, 1 - y][:NY]:
        for d in range(1, NX):
            slot = x_of[d - 1] * NY + yy
            arrive(kbuf.at[slot], k_send.at[d], k_recv.at[slot], x_peers[d - 1])
            arrive(vbuf.at[slot], v_send.at[d], v_recv.at[slot], x_peers[d - 1])

    keys_all = n_kv * ROWS
    keys_up = -(-keys_all // LANES) * LANES
    key_lane = lax.broadcasted_iota(jnp.int32, (1, keys_up), 1)
    live_key = key_lane < 0
    for j in range(n_kv):
        held = lengths[((j // NY) * NZ + z) * NY + j % NY]
        live_key = live_key | ((key_lane >= j * ROWS) & (key_lane < j * ROWS + held))
    spare = [jnp.zeros((keys_up - keys_all, PAIR), F32)] if keys_up > keys_all else []
    stat = jnp.where(lax.rem(lane_row, 8) >= 6, 1.0, 0.0)
    for p in range(pairs):
        query_part = jnp.concatenate(
            [qbuf[j, :, pair_slice(p)].astype(F32) for j in range(NZ)], axis=0
        ).astype(BF16)
        key_part = jnp.concatenate(
            [kbuf[j, :, pair_slice(p)].astype(F32) for j in range(n_kv)] + spare, axis=0
        )
        value_part = jnp.concatenate(
            [vbuf[j, :, pair_slice(p)].astype(F32) for j in range(n_kv)] + spare, axis=0
        ).astype(BF16)
        outs = []
        for which in range(2):
            chosen = first_head if which == 0 else jnp.logical_not(first_head)
            scores = nt(query_part, jnp.where(chosen, key_part, 0.0).astype(BF16)) * 0.125
            scores = jnp.where(live_key, scores, LOW)
            top = jnp.max(scores, axis=1, keepdims=True)
            weights = jnp.exp(scores - top)
            count = jnp.sum(weights, axis=1, keepdims=True)
            outs.append(nn(weights.astype(BF16), value_part))
            head = 2 * p + which
            for j in range(NZ):
                rows = slice(j * ROWS, (j + 1) * ROWS)
                stat = jnp.where(lane_row == j * STATS + head, top[rows], stat)
                stat = jnp.where(lane_row == j * STATS + 8 + head, count[rows], stat)
        mixed = jnp.where(first_head, outs[0], outs[1])
        for j in range(NZ):
            osend[j, :, pair_slice(p)] = mixed[j * ROWS : (j + 1) * ROWS].astype(BF16)
    stat = jnp.concatenate([stat, below], axis=0).T
    for j in range(NZ):
        ssend[j] = stat[j * STATS : (j + 1) * STATS]
    for d in order_z:
        zz = z_of[d - 1]
        send(ssend.at[zz], sbuf.at[z], s_send.at[d], s_recv.at[z], z_peers[d - 1])
        send(osend.at[zz], obuf.at[z], o_send.at[d], o_recv.at[z], z_peers[d - 1])

    for d in range(1, NZ):
        zz = z_of[d - 1]
        arrive(sbuf.at[zz], s_send.at[d], s_recv.at[zz], z_peers[d - 1])
        arrive(obuf.at[zz], o_send.at[d], o_recv.at[zz], z_peers[d - 1])
    sources = [jnp.int32(0) + z] + z_of
    stats = [ssend[z]] + [sbuf[zz] for zz in z_of] + [text_stat]
    top = stats[0][0:8]
    for one in stats[1:]:
        top = jnp.maximum(top, one[0:8])
    factors = [jnp.exp(one[0:8] - top) for one in stats]
    whole = factors[0] * stats[0][8:16]
    for factor, one in zip(factors[1:], stats[1:]):
        whole = whole + factor * one[8:16]
    share = jnp.concatenate(
        [factor / whole for factor in factors]
        + [jnp.zeros((LANES - 8 * len(factors), LANES), F32)],
        axis=0,
    ).T
    attended = []
    for p in range(pairs):
        pieces = [osend[z, :, pair_slice(p)]] + [obuf[zz, :, pair_slice(p)] for zz in z_of]
        pieces = [piece.astype(F32) for piece in pieces] + [text_mixed[p]]
        joined = jnp.zeros((ROWS, PAIR), F32)
        for j, piece in enumerate(pieces):
            lower = share[0:ROWS, 8 * j + 2 * p : 8 * j + 2 * p + 1]
            upper = share[0:ROWS, 8 * j + 2 * p + 1 : 8 * j + 2 * p + 2]
            joined = joined + piece * jnp.where(first_head, lower, upper)
        attended.append(joined.astype(BF16))
    attended = jnp.concatenate(attended, axis=1)

    for copy in load_w:
        copy.wait()
    for d in sorted(range(1, group), reverse=True):
        tt = t_of[d - 1]
        rsend[d - 1] = nn(attended, weight[tt]).astype(BF16)
        send(rsend.at[d - 1], rbuf.at[t], r_send.at[d], r_recv.at[t], t_peers[d - 1])
    summed = nn(attended, weight[t])
    for copy in load_rest:
        copy.wait()
    lifted = 1.0 + scale[...]
    for d in range(1, group):
        tt = t_of[d - 1]
        arrive(rbuf.at[tt], r_send.at[d], r_recv.at[tt], t_peers[d - 1])
        summed = summed + rbuf[tt].astype(F32)
    hidden = stream[...].astype(F32) + gate[...] * summed
    hidden = jnp.where(live_rows[:, 0:1], hidden, 0.0).astype(BF16)
    hidden_out[0] = hidden
    widened = hidden.astype(F32)

    channels = total * PIECE
    tall = ROWS + 8
    extra = jnp.concatenate([lifted, shift[...], jnp.zeros((6, part), F32)], axis=0)
    stacked = jnp.concatenate([widened * lifted, extra], axis=0)
    flipped = nt(proj[...], stacked, lax.Precision.HIGHEST)
    row_sum = nt(jnp.ones((8, part), BF16), hidden)
    row_square = nt(jnp.ones((8, part), F32), widened * widened, lax.Precision.HIGHEST)
    flipped = jnp.concatenate([flipped, jnp.zeros((channels, LANES - tall), F32)], axis=1)
    sums = jnp.where(lax.broadcasted_iota(jnp.int32, (8, ROWS), 0) == 0, row_sum, row_square)
    sums = jnp.concatenate([sums, jnp.zeros((8, LANES - ROWS), F32)], axis=1)
    for g in range(total):
        fsend[g, 0:8, :] = flipped[g * PIECE : (g + 1) * PIECE]
        fsend[g, 8:16, :] = sums
    for d in range(1, total):
        g = g_of[d - 1]
        send(fsend.at[g], fbuf.at[rank], f_send.at[d], f_recv.at[rank], g_peers[d - 1])
    for d in range(1, total):
        g = g_of[d - 1]
        arrive(fbuf.at[g], f_send.at[d], f_recv.at[g], g_peers[d - 1])

    def prediction(half):
        gathered = jnp.zeros((16, LANES), F32)
        for tt in range(group):
            g = half * group + tt
            gathered = gathered + jnp.where(rank == g, fsend[g], fbuf[g])
        mean = gathered[8:9] / D
        square = gathered[9:10] / D
        base = gathered[0:8]
        ratio = lax.rsqrt(square - mean * mean + final_eps)
        lifted_sum = base[:, ROWS : ROWS + 1]
        shift_sum = base[:, ROWS + 1 : ROWS + 2]
        return ratio * (base - mean * lifted_sum) + shift_sum

    conditioned = prediction(0)
    unconditioned = prediction(1)
    guided = unconditioned + guide_scale * (conditioned - unconditioned)
    guided = guided[:, 0:ROWS]
    step = step_index[0]
    current = jnp.zeros((1, ROWS), F32) + alphas[step]
    earlier = jnp.zeros((1, ROWS), F32) + alphas[jnp.maximum(step - STRIDE, 0)]
    root_now = jnp.sqrt(current)
    rest_now = jnp.sqrt(1.0 - current)
    held = latents[...]
    clean = root_now * held - rest_now * guided
    noise = root_now * guided + rest_now * held
    stepped = jnp.sqrt(earlier) * clean + jnp.sqrt(1.0 - earlier) * noise
    token = lax.broadcasted_iota(jnp.int32, (1, ROWS), 1)
    latents_out[...] = jnp.where(token < own_count, stepped, 0.0)

    for copy in sent:
        copy.wait_send()


def shards(
    group,
    stream,
    queries,
    keys,
    values,
    text_keys,
    text_values,
    out_weight,
    gate,
    shift,
    scale,
    proj_weight,
    q_gain,
    k_gain,
    lengths,
    latents,
    alphas,
    step_index,
):
    width = queries.shape[2]
    part = stream.shape[2]
    n_kv = NX * NY
    total = 2 * group
    freq = jnp.asarray(frequencies())
    smem = pl.BlockSpec(memory_space=pltpu.SMEM)
    vmem = pl.BlockSpec(memory_space=pltpu.VMEM)
    anywhere = pl.BlockSpec(memory_space=pl.ANY)
    dma = pltpu.SemaphoreType.DMA
    hidden_out, latents_out = pl.pallas_call(
        functools.partial(kernel, group),
        name="step",
        out_shape=(
            jax.ShapeDtypeStruct((1, ROWS, part), BF16),
            jax.ShapeDtypeStruct((PIECE, ROWS), F32),
        ),
        in_specs=[smem, smem, smem, vmem, vmem, vmem] + [anywhere] * 12,
        out_specs=(vmem, vmem),
        scratch_shapes=[
            pltpu.VMEM((ROWS, width), BF16),
            pltpu.VMEM((ROWS, width), BF16),
            pltpu.VMEM((ROWS, part), BF16),
            pltpu.VMEM((TXT, width), BF16),
            pltpu.VMEM((TXT, width), BF16),
            pltpu.VMEM((group, width, part), BF16),
            pltpu.VMEM((1, part), F32),
            pltpu.VMEM((1, part), F32),
            pltpu.VMEM((1, part), F32),
            pltpu.VMEM((total * PIECE, part), F32),
            pltpu.VMEM((PIECE, ROWS), F32),
            pltpu.VMEM((NZ, ROWS, width), BF16),
            pltpu.VMEM((n_kv, ROWS, width), BF16),
            pltpu.VMEM((n_kv, ROWS, width), BF16),
            pltpu.VMEM((NZ, ROWS, width), BF16),
            pltpu.VMEM((NZ, ROWS, width), BF16),
            pltpu.VMEM((NZ, STATS, LANES), F32),
            pltpu.VMEM((NZ, STATS, LANES), F32),
            pltpu.VMEM((max(group - 1, 1), ROWS, part), BF16),
            pltpu.VMEM((group, ROWS, part), BF16),
            pltpu.VMEM((total, 16, LANES), F32),
            pltpu.VMEM((total, 16, LANES), F32),
            dma((11 + group,)),
            dma((NZ,)),
            dma((NZ,)),
            dma((2 * NX,)),
            dma((n_kv,)),
            dma((2 * NX,)),
            dma((n_kv,)),
            dma((NZ,)),
            dma((NZ,)),
            dma((NZ,)),
            dma((NZ,)),
            dma((group,)),
            dma((group,)),
            dma((total,)),
            dma((total,)),
        ],
        compiler_params=pltpu.CompilerParams(collective_id=0, has_side_effects=True),
    )(
        lengths,
        step_index,
        alphas,
        freq,
        q_gain.reshape(1, HEAD),
        k_gain.reshape(1, HEAD),
        stream,
        queries,
        keys,
        values,
        text_keys,
        text_values,
        out_weight,
        gate.reshape(1, part),
        shift.reshape(1, part),
        scale.reshape(1, part),
        proj_weight.T,
        latents.T,
    )
    return hidden_out, latents_out.T


def solution(mesh):
    return jax.shard_map(
        functools.partial(shards, mesh.shape["tp"]),
        mesh=mesh,
        in_specs=(
            P("cfg", "seq", "tp"),
            P("cfg", "seq", "tp"),
            P("cfg", "seq", "tp"),
            P("cfg", "seq", "tp"),
            P("cfg", None, "tp"),
            P("cfg", None, "tp"),
            P("tp", None),
            P("tp"),
            P("tp"),
            P("tp"),
            P("tp", None),
            P(),
            P(),
            P(),
            P("seq", ("cfg", "tp")),
            P(),
            P(),
        ),
        out_specs=(P("cfg", "seq", "tp"), P("seq", ("cfg", "tp"))),
        check_vma=False,
    )
```

```python
import functools

import jax
import jax.numpy as jnp
import numpy as np
from jax import lax
from jax.experimental import pallas as pl
from jax.experimental.pallas import tpu as pltpu
from jax.sharding import PartitionSpec as P

NX = 4
NZ = 8
NY = 2
D = 3072
HEAD = 64
HP = 30
WP = 45
STRIDE = 20
ROWS = 40
TXT = 226
LANES = 128
PAIR = 2 * HEAD
PIECE = 8
STATS = 16

guide_scale = 6.0
head_eps = 1e-06
final_eps = 1e-05
LOW = -1e30
MESH = pl.DeviceIdType.MESH
F32 = jnp.float32
BF16 = jnp.bfloat16


def frequencies():
    def one(extent):
        return 1.0 / 10000.0 ** (np.arange(0, extent, 2, dtype=np.float32) / np.float32(extent))

    freq = np.concatenate([one(16), one(24), one(24)]).astype(np.float32)
    return np.repeat(freq, 2)[None, :].repeat(2, axis=0).reshape(1, PAIR)


def nt(left, right, precision=None):
    return lax.dot_general(
        left, right, (((1,), (1,)), ((), ())), precision=precision, preferred_element_type=F32
    )


def nn(left, right, precision=None):
    return lax.dot_general(
        left, right, (((1,), (0,)), ((), ())), precision=precision, preferred_element_type=F32
    )


def kernel(
    group,
    lengths_hbm,
    step_index_hbm,
    alphas_hbm,
    freq_hbm,
    q_gain_hbm,
    k_gain_hbm,
    stream_hbm,
    queries_hbm,
    keys_hbm,
    values_hbm,
    text_keys_hbm,
    text_values_hbm,
    weight_hbm,
    gate_hbm,
    shift_hbm,
    scale_hbm,
    proj_hbm,
    latents_hbm,
    hidden_out,
    latents_out,
    lengths,
    step_index,
    alphas,
    freq,
    q_gain,
    k_gain,
    queries,
    keys,
    stream,
    text_keys,
    text_values,
    weight,
    gate,
    shift,
    scale,
    proj,
    latents,
    qbuf,
    kbuf,
    vbuf,
    osend,
    obuf,
    ssend,
    sbuf,
    rsend,
    rbuf,
    fsend,
    fbuf,
    load_sem,
    q_send,
    q_recv,
    k_send,
    k_recv,
    v_send,
    v_recv,
    o_send,
    o_recv,
    s_send,
    s_recv,
    r_send,
    r_recv,
    f_send,
    f_recv,
):
    n_kv = NX * NY
    total = 2 * group
    width = queries.shape[1]
    pairs = width // PAIR
    part = width * 2
    c = lax.axis_index("cfg")
    s = lax.axis_index("seq")
    t = lax.axis_index("tp")
    y = lax.rem(s, NY)
    z = lax.rem(lax.div(s, NY), NZ)
    x = lax.div(s, NY * NZ)
    rank = c * group + t

    def place(xx, zz, yy):
        return (c, (xx * NZ + zz) * NY + yy, t)

    z_of = [lax.rem(z + d, NZ) for d in range(1, NZ)]
    z_peers = [place(x, zz, y) for zz in z_of]
    x_of = [lax.rem(x + d, NX) for d in range(1, NX)]
    x_peers = [place(xx, z, y) for xx in x_of]
    y_peer = place(x, z, 1 - y)
    t_of = [lax.rem(t + d, group) for d in range(1, group)]
    t_peers = [(c, s, tt) for tt in t_of]
    g_of = [lax.rem(rank + d, total) for d in range(1, total)]
    g_peers = [(lax.div(g, group), s, lax.rem(g, group)) for g in g_of]

    barrier = pltpu.get_barrier_semaphore()
    everyone = z_peers + x_peers + ([y_peer] if NY > 1 else []) + g_peers
    for peer in everyone:
        pl.semaphore_signal(barrier, inc=1, device_id=peer, device_id_type=MESH)

    own = x * NY + y
    other = x * NY + (1 - y)

    loads = []

    def load(src, dst):
        copy = pltpu.make_async_copy(src, dst, load_sem.at[len(loads)])
        copy.start()
        loads.append(copy)
        return copy

    load_lengths = load(lengths_hbm, lengths)
    load_k = load(keys_hbm.at[0], keys)
    load_small = [load(freq_hbm, freq), load(q_gain_hbm, q_gain), load(k_gain_hbm, k_gain)]
    load_q = load(queries_hbm.at[0], queries)
    load_v = load(values_hbm.at[0], vbuf.at[own])
    load_tk = load(text_keys_hbm.at[0], text_keys)
    load_tv = load(text_values_hbm.at[0], text_values)
    load_w = [load(weight_hbm.at[:, pl.ds(j * part, part)], weight.at[j]) for j in range(group)]
    load_rest = [
        load(stream_hbm.at[0], stream),
        load(step_index_hbm, step_index),
        load(alphas_hbm, alphas),
        load(gate_hbm, gate),
        load(shift_hbm, shift),
        load(scale_hbm, scale),
        load(proj_hbm, proj),
        load(latents_hbm, latents),
    ]

    load_lengths.wait()
    for copy in load_small:
        copy.wait()
    lane = lax.broadcasted_iota(jnp.int32, (1, PAIR), 1)
    within_head = lax.rem(lane, HEAD)
    is_even = lax.rem(lane, 2) == 0
    first_head = lane < HEAD
    own_start = jnp.int32(0)
    for b in range(NX * NZ * NY):
        own_start = own_start + jnp.where(b < s, lengths[b], 0)
    own_count = lengths[s]
    row = lax.broadcasted_iota(jnp.int32, (ROWS, PAIR), 0)
    live_rows = row < own_count
    position = (row + own_start).astype(F32)
    frame = jnp.floor((position + 0.5) * (1.0 / (HP * WP)))
    line = jnp.floor((position + 0.5) * (1.0 / WP))
    across = position - line * WP
    height = line - frame * HP
    coord = jnp.where(within_head < 16, frame, jnp.where(within_head < 40, height, across))
    angle = coord * freq[...]
    cos_table = jnp.cos(angle)
    sin_table = jnp.sin(angle)
    sin_table = jnp.where(is_even, -sin_table, sin_table)

    r_io = lax.broadcasted_iota(jnp.int32, (PAIR, PAIR), 0)
    c_io = lax.broadcasted_iota(jnp.int32, (PAIR, PAIR), 1)
    mean_matrix = jnp.where((r_io < HEAD) == (c_io < HEAD), 1.0 / HEAD, 0.0)
    mean_matrix_low = mean_matrix.astype(BF16)
    gain_q = q_gain[...].reshape(1, HEAD)
    gain_q = jnp.concatenate([gain_q, gain_q], axis=1)
    gain_k = k_gain[...].reshape(1, HEAD)
    gain_k = jnp.concatenate([gain_k, gain_k], axis=1)

    def head_norm(field, gain):
        centre = field.astype(F32) - nn(field, mean_matrix_low)
        square = centre * centre
        high = square.astype(BF16)
        low = (square - high.astype(F32)).astype(BF16)
        spread = nn(high, mean_matrix_low) + nn(low, mean_matrix_low)
        return centre * lax.rsqrt(spread + head_eps) * gain

    def rotate(field):
        swapped = jnp.where(
            is_even, pltpu.roll(field, PAIR - 1, 1), pltpu.roll(field, 1, 1)
        )
        return field * cos_table + swapped * sin_table

    def pair_slice(p):
        return pl.ds(p * PAIR, PAIR)

    load_k.wait()
    for p in range(pairs):
        made = rotate(head_norm(keys[:, pair_slice(p)], gain_k)).astype(BF16)
        kbuf[own, :, pair_slice(p)] = made
    pl.semaphore_wait(barrier, len(everyone))

    sent = []

    def send(src, dst, send_sem, recv_sem, peer):
        copy = pltpu.make_async_remote_copy(
            src_ref=src,
            dst_ref=dst,
            send_sem=send_sem,
            recv_sem=recv_sem,
            device_id=peer,
            device_id_type=MESH,
        )
        copy.start()
        sent.append(copy)

    def arrive(ref, send_sem, recv_sem, peer):
        pltpu.make_async_remote_copy(
            src_ref=ref,
            dst_ref=ref,
            send_sem=send_sem,
            recv_sem=recv_sem,
            device_id=peer,
            device_id_type=MESH,
        ).wait_recv()

    if NY > 1:
        send(values_hbm.at[0], vbuf.at[own], v_send.at[0], v_recv.at[own], y_peer)
        send(kbuf.at[own], kbuf.at[own], k_send.at[0], k_recv.at[own], y_peer)
    for d in range(1, NX):
        send(values_hbm.at[0], vbuf.at[own], v_send.at[d], v_recv.at[own], x_peers[d - 1])
        send(kbuf.at[own], kbuf.at[own], k_send.at[d], k_recv.at[own], x_peers[d - 1])

    order_z = sorted(range(1, NZ), key=lambda d: -min(d, NZ - d))
    load_q.wait()
    for p in range(pairs):
        made = rotate(head_norm(queries[:, pair_slice(p)], gain_q)).astype(BF16)
        qbuf[z, :, pair_slice(p)] = made

    for d in order_z:
        send(qbuf.at[z], qbuf.at[z], q_send.at[d], q_recv.at[z], z_peers[d - 1])

    load_tk.wait()
    load_tv.wait()
    text_mixed = []
    lane_row = lax.broadcasted_iota(jnp.int32, (ROWS, LANES), 1)
    text_stat = jnp.where(lax.rem(lane_row, 8) >= 6, 1.0, 0.0)
    for p in range(pairs):
        made = head_norm(text_keys[:, pair_slice(p)], gain_k)
        query_part = qbuf[z, :, pair_slice(p)]
        value_part = text_values[:, pair_slice(p)]
        outs = []
        for which in range(2):
            chosen = first_head if which == 0 else jnp.logical_not(first_head)
            key_part = jnp.where(chosen, made, 0.0).astype(BF16)
            scores = nt(query_part, key_part) * 0.125
            top = jnp.max(scores, axis=1, keepdims=True)
            weights = jnp.exp(scores - top)
            count = jnp.sum(weights, axis=1, keepdims=True)
            outs.append(nn(weights.astype(BF16), value_part))
            head = 2 * p + which
            text_stat = jnp.where(lane_row == head, top, text_stat)
            text_stat = jnp.where(lane_row == 8 + head, count, text_stat)
        text_mixed.append(jnp.where(first_head, outs[0], outs[1]))
    below = jnp.zeros((LANES - ROWS, LANES), F32)
    text_stat = jnp.concatenate([text_stat, below], axis=0).T[0:STATS]

    if NY > 1:
        arrive(vbuf.at[other], v_send.at[0], v_recv.at[other], y_peer)
        for d in range(1, NX):
            send(vbuf.at[other], vbuf.at[other], v_send.at[NX - 1 + d], v_recv.at[other], x_peers[d - 1])
        arrive(kbuf.at[other], k_send.at[0], k_recv.at[other], y_peer)
        for d in range(1, NX):
            send(kbuf.at[other], kbuf.at[other], k_send.at[NX - 1 + d], k_recv.at[other], x_peers[d - 1])
    for d in range(1, NZ):
        zz = z_of[d - 1]
        arrive(qbuf.at[zz], q_send.at[d], q_recv.at[zz], z_peers[d - 1])
    for d in range(1, NX):
        slot = x_of[d - 1] * NY + y
        arrive(kbuf.at[slot], k_send.at[d], k_recv.at[slot], x_peers[d - 1])
        arrive(vbuf.at[slot], v_send.at[d], v_recv.at[slot], x_peers[d - 1])
    load_v.wait()

    keys_all = NX * ROWS
    keys_up = -(-keys_all // LANES) * LANES
    key_lane = lax.broadcasted_iota(jnp.int32, (1, keys_up), 1)
    spare = [jnp.zeros((keys_up - keys_all, PAIR), F32)] if keys_up > keys_all else []

    def gather(buf, p, yy):
        blocks = [buf[j * NY + yy, :, pair_slice(p)].astype(F32) for j in range(NX)]
        return jnp.concatenate(blocks + spare, axis=0)

    def live_of(yy):
        live = key_lane < 0
        for j in range(NX):
            held = lengths[(j * NZ + z) * NY + yy]
            live = live | ((key_lane >= j * ROWS) & (key_lane < j * ROWS + held))
        return live

    query_parts = []
    partials = []
    live_key = live_of(y)
    for p in range(pairs):
        query_part = jnp.concatenate(
            [qbuf[j, :, pair_slice(p)].astype(F32) for j in range(NZ)], axis=0
        ).astype(BF16)
        query_parts.append(query_part)
        key_part = gather(kbuf, p, y)
        value_part = gather(vbuf, p, y).astype(BF16)
        for which in range(2):
            chosen = first_head if which == 0 else jnp.logical_not(first_head)
            scores = nt(query_part, jnp.where(chosen, key_part, 0.0).astype(BF16)) * 0.125
            scores = jnp.where(live_key, scores, LOW)
            top = jnp.max(scores, axis=1, keepdims=True)
            weights = jnp.exp(scores - top)
            count = jnp.sum(weights, axis=1, keepdims=True)
            partials.append((top, count, nn(weights.astype(BF16), value_part)))

    if NY > 1:
        for d in range(1, NX):
            slot = x_of[d - 1] * NY + 1 - y
            arrive(kbuf.at[slot], k_send.at[d], k_recv.at[slot], x_peers[d - 1])
            arrive(vbuf.at[slot], v_send.at[d], v_recv.at[slot], x_peers[d - 1])
    stat = jnp.where(lax.rem(lane_row, 8) >= 6, 1.0, 0.0)
    live_key = live_of(1 - y)
    for p in range(pairs):
        if NY > 1:
            key_part = gather(kbuf, p, 1 - y)
            value_part = gather(vbuf, p, 1 - y).astype(BF16)
        outs = []
        for which in range(2):
            head = 2 * p + which
            top, count, out = partials[head]
            if NY > 1:
                chosen = first_head if which == 0 else jnp.logical_not(first_head)
                scores = nt(query_parts[p], jnp.where(chosen, key_part, 0.0).astype(BF16)) * 0.125
                scores = jnp.where(live_key, scores, LOW)
                before = top
                top = jnp.maximum(before, jnp.max(scores, axis=1, keepdims=True))
                fade = jnp.exp(before - top)
                weights = jnp.exp(scores - top)
                count = count * fade + jnp.sum(weights, axis=1, keepdims=True)
                out = out * fade + nn(weights.astype(BF16), value_part)
            outs.append(out)
            for j in range(NZ):
                rows = slice(j * ROWS, (j + 1) * ROWS)
                stat = jnp.where(lane_row == j * STATS + head, top[rows], stat)
                stat = jnp.where(lane_row == j * STATS + 8 + head, count[rows], stat)
        mixed = jnp.where(first_head, outs[0], outs[1])
        for j in range(NZ):
            osend[p, j] = mixed[j * ROWS : (j + 1) * ROWS].astype(BF16)
        if p == pairs - 1:
            flat = jnp.concatenate([stat, below], axis=0).T
            for j in range(NZ):
                tops = flat[j * STATS : j * STATS + 8]
                counts = flat[j * STATS + 8 : j * STATS + 16]
                ssend[j] = tops + pltpu.roll(counts, HEAD, 1)
            for d in order_z:
                zz = z_of[d - 1]
                send(ssend.at[zz], sbuf.at[z], s_send.at[d], s_recv.at[z], z_peers[d - 1])
        for d in order_z:
            zz = z_of[d - 1]
            send(osend.at[p, zz], obuf.at[p, z], o_send.at[p, d], o_recv.at[p, z], z_peers[d - 1])

    for d in range(1, NZ):
        zz = z_of[d - 1]
        arrive(sbuf.at[zz], s_send.at[d], s_recv.at[zz], z_peers[d - 1])
        for p in range(pairs):
            arrive(obuf.at[p, zz], o_send.at[p, d], o_recv.at[p, zz], z_peers[d - 1])
    tiles = [ssend[z]] + [sbuf[zz] for zz in z_of]
    tops = tiles + [text_stat[0:8]]
    counts = [pltpu.roll(tile, HEAD, 1) for tile in tiles] + [text_stat[8:16]]
    top = functools.reduce(jnp.maximum, tops)
    factors = [jnp.exp(one - top) for one in tops]
    whole = sum(factor * count for factor, count in zip(factors, counts))
    share = jnp.concatenate(
        [factor / whole for factor in factors]
        + [jnp.zeros((LANES - 8 * len(factors), LANES), F32)],
        axis=0,
    ).T
    attended = []
    for p in range(pairs):
        pieces = [osend[p, z]] + [obuf[p, zz] for zz in z_of]
        pieces = [piece.astype(F32) for piece in pieces] + [text_mixed[p]]
        joined = jnp.zeros((ROWS, PAIR), F32)
        for j, piece in enumerate(pieces):
            lower = share[0:ROWS, 8 * j + 2 * p : 8 * j + 2 * p + 1]
            upper = share[0:ROWS, 8 * j + 2 * p + 1 : 8 * j + 2 * p + 2]
            joined = joined + piece * jnp.where(first_head, lower, upper)
        attended.append(joined.astype(BF16))
    attended = jnp.concatenate(attended, axis=1)

    for copy in load_w:
        copy.wait()
    for d in sorted(range(1, group), reverse=True):
        tt = t_of[d - 1]
        rsend[d - 1] = nn(attended, weight[tt]).astype(BF16)
        send(rsend.at[d - 1], rbuf.at[t], r_send.at[d], r_recv.at[t], t_peers[d - 1])
    summed = nn(attended, weight[t])
    for copy in load_rest:
        copy.wait()
    lifted = 1.0 + scale[...].reshape(1, part)
    for d in range(1, group):
        tt = t_of[d - 1]
        arrive(rbuf.at[tt], r_send.at[d], r_recv.at[tt], t_peers[d - 1])
        summed = summed + rbuf[tt].astype(F32)
    hidden = stream[...].astype(F32) + gate[...].reshape(1, part) * summed
    hidden = jnp.where(live_rows[:, 0:1], hidden, 0.0).astype(BF16)
    hidden_out[0] = hidden
    widened = hidden.astype(F32)

    channels = total * PIECE
    tall = ROWS + 8
    extra = jnp.concatenate([lifted, shift[...].reshape(1, part), jnp.zeros((6, part), F32)], axis=0)
    stacked = jnp.concatenate([widened * lifted, extra], axis=0)
    flipped = nt(proj[...], stacked, lax.Precision.HIGHEST)
    row_sum = nt(jnp.ones((8, part), BF16), hidden)
    row_square = nt(jnp.ones((8, part), F32), widened * widened, lax.Precision.HIGHEST)
    flipped = jnp.concatenate([flipped, jnp.zeros((channels, HEAD - tall), F32)], axis=1)
    sums = jnp.where(lax.broadcasted_iota(jnp.int32, (8, ROWS), 0) == 0, row_sum, row_square)
    sums = jnp.concatenate([sums, jnp.zeros((8, HEAD - ROWS), F32)], axis=1)
    for g in range(total):
        fsend[g] = jnp.concatenate([flipped[g * PIECE : (g + 1) * PIECE], sums], axis=1)
    for d in range(1, total):
        g = g_of[d - 1]
        send(fsend.at[g], fbuf.at[rank], f_send.at[d], f_recv.at[rank], g_peers[d - 1])
    for d in range(1, total):
        g = g_of[d - 1]
        arrive(fbuf.at[g], f_send.at[d], f_recv.at[g], g_peers[d - 1])

    def prediction(half):
        gathered = jnp.zeros((8, LANES), F32)
        for tt in range(group):
            g = half * group + tt
            gathered = gathered + jnp.where(rank == g, fsend[g], fbuf[g])
        sums = pltpu.roll(gathered, HEAD, 1)
        mean = sums[0:1] / D
        square = sums[1:2] / D
        base = gathered
        ratio = lax.rsqrt(square - mean * mean + final_eps)
        lifted_sum = base[:, ROWS : ROWS + 1]
        shift_sum = base[:, ROWS + 1 : ROWS + 2]
        return ratio * (base - mean * lifted_sum) + shift_sum

    conditioned = prediction(0)
    unconditioned = prediction(1)
    guided = unconditioned + guide_scale * (conditioned - unconditioned)
    guided = guided[:, 0:ROWS]
    step = step_index[0]
    current = jnp.zeros((1, ROWS), F32) + alphas[step]
    earlier = jnp.zeros((1, ROWS), F32) + alphas[jnp.maximum(step - STRIDE, 0)]
    root_now = jnp.sqrt(current)
    rest_now = jnp.sqrt(1.0 - current)
    held = latents[...]
    clean = root_now * held - rest_now * guided
    noise = root_now * guided + rest_now * held
    stepped = jnp.sqrt(earlier) * clean + jnp.sqrt(1.0 - earlier) * noise
    token = lax.broadcasted_iota(jnp.int32, (1, ROWS), 1)
    latents_out[...] = jnp.where(token < own_count, stepped, 0.0)

    for copy in sent:
        copy.wait_send()


def finish_kernel(hidden, latents, hidden_out, latents_out, sem):
    copies = [
        pltpu.make_async_copy(hidden, hidden_out, sem.at[0]),
        pltpu.make_async_copy(latents, latents_out, sem.at[1]),
    ]
    for copy in copies:
        copy.start()
    for copy in copies:
        copy.wait()


def finish(hidden, latents):
    vmem = pl.BlockSpec(memory_space=pltpu.VMEM)
    anywhere = pl.BlockSpec(memory_space=pl.ANY)
    hidden, latents = pl.pallas_call(
        finish_kernel,
        name="finish",
        out_shape=(
            jax.ShapeDtypeStruct(hidden.shape, hidden.dtype),
            jax.ShapeDtypeStruct(latents.shape, latents.dtype),
        ),
        in_specs=[vmem, vmem],
        out_specs=(anywhere, anywhere),
        scratch_shapes=[pltpu.SemaphoreType.DMA((2,))],
    )(hidden, latents)
    return hidden, latents.T


def shards(
    group,
    stream,
    queries,
    keys,
    values,
    text_keys,
    text_values,
    out_weight,
    gate,
    shift,
    scale,
    proj_weight,
    q_gain,
    k_gain,
    lengths,
    latents,
    alphas,
    step_index,
):
    width = queries.shape[2]
    part = stream.shape[2]
    n_kv = NX * NY
    total = 2 * group
    freq = jnp.asarray(frequencies())
    vmem = pl.BlockSpec(memory_space=pltpu.VMEM)
    anywhere = pl.BlockSpec(memory_space=pl.ANY)
    dma = pltpu.SemaphoreType.DMA
    hidden_out, latents_out = pl.pallas_call(
        functools.partial(kernel, group),
        name="step",
        out_shape=(
            jax.ShapeDtypeStruct((1, ROWS, part), BF16),
            jax.ShapeDtypeStruct((PIECE, ROWS), F32),
        ),
        in_specs=[anywhere] * 18,
        out_specs=(vmem, vmem),
        scratch_shapes=[
            pltpu.SMEM((NX * NZ * NY,), jnp.int32),
            pltpu.SMEM((1,), jnp.int32),
            pltpu.SMEM((alphas.shape[0],), F32),
            pltpu.VMEM((1, PAIR), F32),
            pltpu.VMEM((HEAD,), F32),
            pltpu.VMEM((HEAD,), F32),
            pltpu.VMEM((ROWS, width), BF16),
            pltpu.VMEM((ROWS, width), BF16),
            pltpu.VMEM((ROWS, part), BF16),
            pltpu.VMEM((TXT, width), BF16),
            pltpu.VMEM((TXT, width), BF16),
            pltpu.VMEM((group, width, part), BF16),
            pltpu.VMEM((part,), F32),
            pltpu.VMEM((part,), F32),
            pltpu.VMEM((part,), F32),
            pltpu.VMEM((total * PIECE, part), F32),
            pltpu.VMEM((PIECE, ROWS), F32),
            pltpu.VMEM((NZ, ROWS, width), BF16),
            pltpu.VMEM((n_kv, ROWS, width), BF16),
            pltpu.VMEM((n_kv, ROWS, width), BF16),
            pltpu.VMEM((width // PAIR, NZ, ROWS, PAIR), BF16),
            pltpu.VMEM((width // PAIR, NZ, ROWS, PAIR), BF16),
            pltpu.VMEM((NZ, 8, LANES), F32),
            pltpu.VMEM((NZ, 8, LANES), F32),
            pltpu.VMEM((max(group - 1, 1), ROWS, part), BF16),
            pltpu.VMEM((group, ROWS, part), BF16),
            pltpu.VMEM((total, 8, LANES), F32),
            pltpu.VMEM((total, 8, LANES), F32),
            dma((17 + group,)),
            dma((NZ,)),
            dma((NZ,)),
            dma((2 * NX,)),
            dma((n_kv,)),
            dma((2 * NX,)),
            dma((n_kv,)),
            dma((width // PAIR, NZ)),
            dma((width // PAIR, NZ)),
            dma((NZ,)),
            dma((NZ,)),
            dma((group,)),
            dma((group,)),
            dma((total,)),
            dma((total,)),
        ],
        compiler_params=pltpu.CompilerParams(collective_id=0, has_side_effects=True),
    )(
        lengths,
        step_index,
        alphas,
        freq,
        q_gain,
        k_gain,
        stream,
        queries,
        keys,
        values,
        text_keys,
        text_values,
        out_weight,
        gate,
        shift,
        scale,
        proj_weight.T,
        latents.T,
    )
    return finish(hidden_out, latents_out)


def solution(mesh):
    return jax.shard_map(
        functools.partial(shards, mesh.shape["tp"]),
        mesh=mesh,
        in_specs=(
            P("cfg", "seq", "tp"),
            P("cfg", "seq", "tp"),
            P("cfg", "seq", "tp"),
            P("cfg", "seq", "tp"),
            P("cfg", None, "tp"),
            P("cfg", None, "tp"),
            P("tp", None),
            P("tp"),
            P("tp"),
            P("tp"),
            P("tp", None),
            P(),
            P(),
            P(),
            P("seq", ("cfg", "tp")),
            P(),
            P(),
        ),
        out_specs=(P("cfg", "seq", "tp"), P("seq", ("cfg", "tp"))),
        check_vma=False,
    )
```

```python
import functools

import jax
import jax.numpy as jnp
import numpy as np
from jax import lax
from jax.experimental import pallas as pl
from jax.experimental.pallas import tpu as pltpu
from jax.sharding import PartitionSpec as P

NX = 4
NZ = 8
NY = 2
D = 3072
HEAD = 64
HP = 30
WP = 45
STRIDE = 20
ROWS = 40
TXT = 226
LANES = 128
PAIR = 2 * HEAD
PIECE = 8
STATS = 16

guide_scale = 6.0
head_eps = 1e-06
final_eps = 1e-05
LOW = -1e30
QUERY, NEAR, OTHER_V, OTHER_K, FAR, STAT, OUT, PART, LAST = range(9)
MESH = pl.DeviceIdType.MESH
F32 = jnp.float32
BF16 = jnp.bfloat16


def frequencies():
    def one(extent):
        return 1.0 / 10000.0 ** (np.arange(0, extent, 2, dtype=np.float32) / np.float32(extent))

    freq = np.concatenate([one(16), one(24), one(24)]).astype(np.float32)
    return np.repeat(freq, 2)[None, :].repeat(2, axis=0).reshape(1, PAIR)


def nt(left, right, precision=None):
    return lax.dot_general(
        left, right, (((1,), (1,)), ((), ())), precision=precision, preferred_element_type=F32
    )


def nn(left, right, precision=None):
    return lax.dot_general(
        left, right, (((1,), (0,)), ((), ())), precision=precision, preferred_element_type=F32
    )


def kernel(
    group,
    lengths_hbm,
    step_index_hbm,
    alphas_hbm,
    freq_hbm,
    q_gain_hbm,
    k_gain_hbm,
    stream_hbm,
    queries_hbm,
    keys_hbm,
    values_hbm,
    text_keys_hbm,
    text_values_hbm,
    weight_hbm,
    gate_hbm,
    shift_hbm,
    scale_hbm,
    proj_hbm,
    latents_hbm,
    hidden_out,
    latents_out,
    lengths,
    step_index,
    alphas,
    freq,
    q_gain,
    k_gain,
    queries,
    keys,
    stream,
    text_keys,
    text_values,
    weight,
    gate,
    shift,
    scale,
    proj,
    latents,
    qbuf,
    kbuf,
    vbuf,
    osend,
    obuf,
    ssend,
    sbuf,
    rsend,
    rbuf,
    fsend,
    fbuf,
    load_sem,
    send_sem,
    recv_sem,
):
    n_kv = NX * NY
    total = 2 * group
    width = queries.shape[1]
    pairs = width // PAIR
    part = width * 2
    c = lax.axis_index("cfg")
    s = lax.axis_index("seq")
    t = lax.axis_index("tp")
    y = lax.rem(s, NY)
    z = lax.rem(lax.div(s, NY), NZ)
    x = lax.div(s, NY * NZ)
    rank = c * group + t

    def place(xx, zz, yy):
        return (c, (xx * NZ + zz) * NY + yy, t)

    z_of = [lax.rem(z + d, NZ) for d in range(1, NZ)]
    z_peers = [place(x, zz, y) for zz in z_of]
    x_of = [lax.rem(x + d, NX) for d in range(1, NX)]
    x_peers = [place(xx, z, y) for xx in x_of]
    y_peer = place(x, z, 1 - y)
    t_of = [t + 1 - 2 * lax.rem(t, 2), lax.rem(t + 2, group), group - 1 - t][: group - 1]
    t_peers = [(c, s, tt) for tt in t_of]
    g_of = [lax.rem(rank + d, total) for d in range(1, total)]
    g_peers = [(lax.div(g, group), s, lax.rem(g, group)) for g in g_of]

    barrier = pltpu.get_barrier_semaphore()
    everyone = z_peers + x_peers + ([y_peer] if NY > 1 else []) + g_peers
    for peer in everyone:
        pl.semaphore_signal(barrier, inc=1, device_id=peer, device_id_type=MESH)

    own = x * NY + y
    other = x * NY + (1 - y)

    def load(src, dst, which):
        copy = pltpu.make_async_copy(src, dst, load_sem.at[which])
        copy.start()
        return copy

    load_small = [
        load(lengths_hbm, lengths, 0),
        load(freq_hbm, freq, 1),
        load(q_gain_hbm, q_gain, 2),
        load(k_gain_hbm, k_gain, 3),
    ]
    load_k = load(keys_hbm.at[0], keys, 4)
    load_q = load(queries_hbm.at[0], queries, 5)
    load_v = load(values_hbm.at[0], vbuf.at[own], 6)
    load_text = [load(text_keys_hbm.at[0], text_keys, 7), load(text_values_hbm.at[0], text_values, 8)]
    for j in range(group):
        load(weight_hbm.at[:, pl.ds(j * part, part)], weight.at[j], 9)
    load_rest = [
        load(step_index_hbm, step_index, 10),
        load(alphas_hbm, alphas, 11),
        load(stream_hbm.at[0], stream, 12),
        load(gate_hbm, gate, 13),
        load(shift_hbm, shift, 14),
        load(scale_hbm, scale, 15),
        load(proj_hbm, proj, 16),
        load(latents_hbm, latents, 17),
    ]

    for copy in load_small:
        copy.wait()
    lane = lax.broadcasted_iota(jnp.int32, (1, PAIR), 1)
    within_head = lax.rem(lane, HEAD)
    is_even = lax.rem(lane, 2) == 0
    first_head = lane < HEAD
    own_start = jnp.int32(0)
    for b in range(NX * NZ * NY):
        own_start = own_start + jnp.where(b < s, lengths[b], 0)
    own_count = lengths[s]
    row = lax.broadcasted_iota(jnp.int32, (ROWS, PAIR), 0)
    live_rows = row < own_count
    position = (row + own_start).astype(F32)
    frame = jnp.floor((position + 0.5) * (1.0 / (HP * WP)))
    line = jnp.floor((position + 0.5) * (1.0 / WP))
    across = position - line * WP
    height = line - frame * HP
    coord = jnp.where(within_head < 16, frame, jnp.where(within_head < 40, height, across))
    angle = coord * freq[...]
    cos_table = jnp.cos(angle)
    sin_table = jnp.sin(angle)
    sin_table = jnp.where(is_even, -sin_table, sin_table)

    r_io = lax.broadcasted_iota(jnp.int32, (PAIR, PAIR), 0)
    c_io = lax.broadcasted_iota(jnp.int32, (PAIR, PAIR), 1)
    mean_matrix = jnp.where((r_io < HEAD) == (c_io < HEAD), 1.0 / HEAD, 0.0)
    mean_matrix_low = mean_matrix.astype(BF16)
    gain_q = q_gain[...].reshape(1, HEAD)
    gain_q = jnp.concatenate([gain_q, gain_q], axis=1)
    gain_k = k_gain[...].reshape(1, HEAD)
    gain_k = jnp.concatenate([gain_k, gain_k], axis=1)

    def head_norm(field, gain):
        centre = field.astype(F32) - nn(field, mean_matrix_low)
        square = centre * centre
        high = square.astype(BF16)
        low = (square - high.astype(F32)).astype(BF16)
        spread = nn(high, mean_matrix_low) + nn(low, mean_matrix_low)
        return centre * lax.rsqrt(spread + head_eps) * gain

    def rotate(field):
        swapped = jnp.where(
            is_even, pltpu.roll(field, PAIR - 1, 1), pltpu.roll(field, 1, 1)
        )
        return field * cos_table + swapped * sin_table

    def pair_slice(p):
        return pl.ds(p * PAIR, PAIR)

    load_k.wait()
    for p in range(pairs):
        made = rotate(head_norm(keys[:, pair_slice(p)], gain_k)).astype(BF16)
        kbuf[own, :, pair_slice(p)] = made
    pl.semaphore_wait(barrier, len(everyone))

    def send(src, dst, kind, which, peer):
        copy = pltpu.make_async_remote_copy(
            src_ref=src,
            dst_ref=dst,
            send_sem=send_sem.at[kind],
            recv_sem=recv_sem.at[which],
            device_id=peer,
            device_id_type=MESH,
        )
        copy.start()

    def whole_copy(ref, kind, which):
        return pltpu.make_async_remote_copy(
            src_ref=ref,
            dst_ref=ref,
            send_sem=send_sem.at[kind],
            recv_sem=recv_sem.at[which],
            device_id=g_peers[0],
            device_id_type=MESH,
        )

    def arrive(ref, which):
        whole_copy(ref, 0, which).wait_recv()

    if NY > 1:
        send(values_hbm.at[0], vbuf.at[own], 1, OTHER_V, y_peer)
        send(kbuf.at[own], kbuf.at[own], 0, OTHER_K, y_peer)
    for d in range(1, NX):
        send(values_hbm.at[0], vbuf.at[own], 1, NEAR, x_peers[d - 1])
        send(kbuf.at[own], kbuf.at[own], 0, NEAR, x_peers[d - 1])

    order_z = sorted(range(1, NZ), key=lambda d: -min(d, NZ - d))
    load_q.wait()
    for p in range(pairs):
        made = rotate(head_norm(queries[:, pair_slice(p)], gain_q)).astype(BF16)
        qbuf[z, :, pair_slice(p)] = made

    for d in order_z:
        send(qbuf.at[z], qbuf.at[z], 2, QUERY, z_peers[d - 1])

    for copy in load_text:
        copy.wait()
    text_mixed = []
    lane_row = lax.broadcasted_iota(jnp.int32, (ROWS, LANES), 1)
    text_stat = jnp.where(lax.rem(lane_row, 8) >= 6, 1.0, 0.0)
    for p in range(pairs):
        made = head_norm(text_keys[:, pair_slice(p)], gain_k)
        query_part = qbuf[z, :, pair_slice(p)]
        value_part = text_values[:, pair_slice(p)]
        outs = []
        for which in range(2):
            chosen = first_head if which == 0 else jnp.logical_not(first_head)
            key_part = jnp.where(chosen, made, 0.0).astype(BF16)
            scores = nt(query_part, key_part) * 0.125
            top = jnp.max(scores, axis=1, keepdims=True)
            weights = jnp.exp(scores - top)
            count = jnp.sum(weights, axis=1, keepdims=True)
            outs.append(nn(weights.astype(BF16), value_part))
            head = 2 * p + which
            text_stat = jnp.where(lane_row == head, top, text_stat)
            text_stat = jnp.where(lane_row == 8 + head, count, text_stat)
        text_mixed.append(jnp.where(first_head, outs[0], outs[1]))
    below = jnp.zeros((LANES - ROWS, LANES), F32)
    text_stat = jnp.concatenate([text_stat, below], axis=0).T[0:STATS]

    if NY > 1:
        arrive(vbuf.at[other], OTHER_V)
        for d in range(1, NX):
            send(vbuf.at[other], vbuf.at[other], 1, FAR, x_peers[d - 1])
        arrive(kbuf.at[other], OTHER_K)
        for d in range(1, NX):
            send(kbuf.at[other], kbuf.at[other], 0, FAR, x_peers[d - 1])
    arrive(qbuf.at[pl.ds(0, NZ - 1)], QUERY)
    arrive(kbuf.at[pl.ds(0, 2 * (NX - 1))], NEAR)
    load_v.wait()

    n_keys = NX * ROWS
    n_queries = NZ * ROWS
    q_up = -(-n_queries // LANES) * LANES
    slot_row = lax.broadcasted_iota(jnp.int32, (ROWS, 1), 0)

    def gather(buf, p, yy):
        blocks = [buf[j * NY + yy, :, pair_slice(p)].astype(F32) for j in range(NX)]
        return jnp.concatenate(blocks, axis=0)

    def live_of(yy):
        pieces = [
            jnp.where(slot_row < lengths[(j * NZ + z) * NY + yy], 0.0, LOW) for j in range(NX)
        ]
        return jnp.concatenate(pieces + pieces, axis=0)

    def score(p, yy, live):
        key_part = gather(kbuf, p, yy)
        both = jnp.concatenate(
            [jnp.where(first_head, key_part, 0.0), jnp.where(first_head, 0.0, key_part)], axis=0
        ).astype(BF16)
        found = jnp.where(live < 0.0, LOW, nt(both, query_parts[p]) * 0.125)
        turned = gather(vbuf, p, yy).T.astype(BF16)
        return [
            (found[w * n_keys : (w + 1) * n_keys], turned[w * HEAD : (w + 1) * HEAD])
            for w in range(2)
        ]

    query_parts = []
    partials = []
    live = live_of(y)
    for p in range(pairs):
        query_parts.append(
            jnp.concatenate(
                [qbuf[j, :, pair_slice(p)].astype(F32) for j in range(NZ)], axis=0
            ).astype(BF16)
        )
    near = [score(p, y, live) for p in range(pairs)]
    for p in range(pairs):
        for scores, turned in near[p]:
            top = jnp.max(scores, axis=0, keepdims=True)
            weights = jnp.exp(scores - top)
            count = jnp.sum(weights, axis=0, keepdims=True)
            partials.append((top, count, nn(turned, weights.astype(BF16))))

    if NY > 1:
        arrive(kbuf.at[pl.ds(0, 2 * (NX - 1))], FAR)
    live = live_of(1 - y)
    stat_row = lax.broadcasted_iota(jnp.int32, (8, q_up), 0)
    tops = jnp.zeros((8, q_up), F32)
    counts = jnp.ones((8, q_up), F32)
    lane_tile = lax.broadcasted_iota(jnp.int32, (8, LANES), 1)

    def widen(line):
        if q_up == n_queries:
            return line
        return jnp.concatenate([line, jnp.zeros((line.shape[0], q_up - n_queries), F32)], axis=1)

    far = [score(p, 1 - y, live) for p in range(pairs)] if NY > 1 else None
    for p in range(pairs):
        outs = []
        for which in range(2):
            head = 2 * p + which
            top, count, out = partials[head]
            if NY > 1:
                scores, turned = far[p][which]
                before = top
                top = jnp.maximum(before, jnp.max(scores, axis=0, keepdims=True))
                fade = jnp.exp(before - top)
                weights = jnp.exp(scores - top)
                count = count * fade + jnp.sum(weights, axis=0, keepdims=True)
                out = out * fade + nn(turned, weights.astype(BF16))
            outs.append(out)
            tops = jnp.where(stat_row == head, widen(top), tops)
            counts = jnp.where(stat_row == head, widen(count), counts)
        mixed = widen(jnp.concatenate(outs, axis=0)).T
        for j in range(NZ):
            osend[p, j] = mixed[j * ROWS : (j + 1) * ROWS].astype(BF16)
        if p == pairs - 1:
            for j in range(NZ):
                left = pltpu.roll(tops, (q_up - j * ROWS) % q_up, 1)[:, 0:LANES]
                right = pltpu.roll(counts, (q_up + HEAD - j * ROWS) % q_up, 1)[:, 0:LANES]
                ssend[j] = jnp.where(lane_tile < HEAD, left, right)
            for d in order_z:
                zz = z_of[d - 1]
                send(ssend.at[zz], sbuf.at[z], 3, STAT, z_peers[d - 1])
        for d in order_z:
            zz = z_of[d - 1]
            send(osend.at[p, zz], obuf.at[p, z], 4, OUT, z_peers[d - 1])

    arrive(sbuf.at[pl.ds(0, NZ - 1)], STAT)
    arrive(obuf.at[:, pl.ds(0, NZ - 1)], OUT)
    tiles = [ssend[z]] + [sbuf[zz] for zz in z_of]
    tops = tiles + [text_stat[0:8]]
    counts = [pltpu.roll(tile, HEAD, 1) for tile in tiles] + [text_stat[8:16]]
    top = functools.reduce(jnp.maximum, tops)
    factors = [jnp.exp(one - top) for one in tops]
    whole = sum(factor * count for factor, count in zip(factors, counts))
    share = jnp.concatenate(
        [factor / whole for factor in factors]
        + [jnp.zeros((LANES - 8 * len(factors), LANES), F32)],
        axis=0,
    ).T
    attended = []
    for p in range(pairs):
        pieces = [osend[p, z]] + [obuf[p, zz] for zz in z_of]
        pieces = [piece.astype(F32) for piece in pieces] + [text_mixed[p]]
        joined = jnp.zeros((ROWS, PAIR), F32)
        for j, piece in enumerate(pieces):
            lower = share[0:ROWS, 8 * j + 2 * p : 8 * j + 2 * p + 1]
            upper = share[0:ROWS, 8 * j + 2 * p + 1 : 8 * j + 2 * p + 2]
            joined = joined + piece * jnp.where(first_head, lower, upper)
        attended.append(joined.astype(BF16))
    attended = jnp.concatenate(attended, axis=1)

    pltpu.make_async_copy(weight, weight, load_sem.at[9]).wait()
    for d in sorted(range(1, group), reverse=True):
        tt = t_of[d - 1]
        rsend[d - 1] = nn(attended, weight[tt]).astype(BF16)
        send(rsend.at[d - 1], rbuf.at[t], 5, PART, t_peers[d - 1])
    summed = nn(attended, weight[t])
    for copy in load_rest:
        copy.wait()
    lifted = 1.0 + scale[...].reshape(1, part)
    arrive(rbuf.at[pl.ds(0, group - 1)], PART)
    for tt in t_of:
        summed = summed + rbuf[tt].astype(F32)
    hidden = stream[...].astype(F32) + gate[...].reshape(1, part) * summed
    hidden = jnp.where(live_rows[:, 0:1], hidden, 0.0).astype(BF16)
    hidden_out[0] = hidden
    widened = hidden.astype(F32)

    channels = total * PIECE
    tall = ROWS + 8
    extra = jnp.concatenate([lifted, shift[...].reshape(1, part), jnp.zeros((6, part), F32)], axis=0)
    stacked = jnp.concatenate([widened * lifted, extra], axis=0)
    flipped = nt(proj[...], stacked, lax.Precision.HIGHEST)
    row_sum = nt(jnp.ones((8, part), BF16), hidden)
    row_square = nt(jnp.ones((8, part), F32), widened * widened, lax.Precision.HIGHEST)
    flipped = jnp.concatenate([flipped, jnp.zeros((channels, HEAD - tall), F32)], axis=1)
    sums = jnp.where(lax.broadcasted_iota(jnp.int32, (8, ROWS), 0) == 0, row_sum, row_square)
    sums = jnp.concatenate([sums, jnp.zeros((8, HEAD - ROWS), F32)], axis=1)
    for g in range(total):
        fsend[g] = jnp.concatenate([flipped[g * PIECE : (g + 1) * PIECE], sums], axis=1)
    for d in range(1, total):
        g = g_of[d - 1]
        send(fsend.at[g], fbuf.at[rank], 6, LAST, g_peers[d - 1])
    arrive(fbuf.at[pl.ds(0, total - 1)], LAST)

    def prediction(half):
        gathered = jnp.zeros((8, LANES), F32)
        for tt in range(group):
            g = half * group + tt
            gathered = gathered + jnp.where(rank == g, fsend[g], fbuf[g])
        sums = pltpu.roll(gathered, HEAD, 1)
        mean = sums[0:1] / D
        square = sums[1:2] / D
        base = gathered
        ratio = lax.rsqrt(square - mean * mean + final_eps)
        lifted_sum = base[:, ROWS : ROWS + 1]
        shift_sum = base[:, ROWS + 1 : ROWS + 2]
        return ratio * (base - mean * lifted_sum) + shift_sum

    conditioned = prediction(0)
    unconditioned = prediction(1)
    guided = unconditioned + guide_scale * (conditioned - unconditioned)
    guided = guided[:, 0:ROWS]
    step = step_index[0, 0]
    current = jnp.zeros((1, ROWS), F32) + alphas[step]
    earlier = jnp.zeros((1, ROWS), F32) + alphas[jnp.maximum(step - STRIDE, 0)]
    root_now = jnp.sqrt(current)
    rest_now = jnp.sqrt(1.0 - current)
    held = latents[...]
    clean = root_now * held - rest_now * guided
    noise = root_now * guided + rest_now * held
    stepped = jnp.sqrt(earlier) * clean + jnp.sqrt(1.0 - earlier) * noise
    token = lax.broadcasted_iota(jnp.int32, (1, ROWS), 1)
    latents_out[...] = jnp.where(token < own_count, stepped, 0.0)

    n_block = NX - 1 + (NX if NY > 1 else 0)
    for kind, ref in enumerate(
        [
            kbuf.at[pl.ds(0, n_block)],
            vbuf.at[pl.ds(0, n_block)],
            qbuf.at[pl.ds(0, NZ - 1)],
            sbuf.at[pl.ds(0, NZ - 1)],
            obuf.at[:, pl.ds(0, NZ - 1)],
            rbuf.at[pl.ds(0, group - 1)],
            fbuf.at[pl.ds(0, total - 1)],
        ]
    ):
        whole_copy(ref, kind, 0).wait_send()


def finish_kernel(hidden, latents, hidden_out, latents_out, sem):
    copies = [
        pltpu.make_async_copy(hidden, hidden_out, sem.at[0]),
        pltpu.make_async_copy(latents, latents_out, sem.at[1]),
    ]
    for copy in copies:
        copy.start()
    for copy in copies:
        copy.wait()


def finish(hidden, latents):
    vmem = pl.BlockSpec(memory_space=pltpu.VMEM)
    anywhere = pl.BlockSpec(memory_space=pl.ANY)
    hidden, latents = pl.pallas_call(
        finish_kernel,
        name="finish",
        out_shape=(
            jax.ShapeDtypeStruct(hidden.shape, hidden.dtype),
            jax.ShapeDtypeStruct(latents.shape, latents.dtype),
        ),
        in_specs=[vmem, vmem],
        out_specs=(anywhere, anywhere),
        scratch_shapes=[pltpu.SemaphoreType.DMA((2,))],
    )(
        pltpu.with_memory_space_constraint(hidden, pltpu.VMEM),
        pltpu.with_memory_space_constraint(latents, pltpu.VMEM),
    )
    return hidden, latents.T


def shards(
    group,
    stream,
    queries,
    keys,
    values,
    text_keys,
    text_values,
    out_weight,
    gate,
    shift,
    scale,
    proj_weight,
    q_gain,
    k_gain,
    lengths,
    latents,
    alphas,
    step_index,
):
    width = queries.shape[2]
    part = stream.shape[2]
    n_kv = NX * NY
    total = 2 * group
    freq = jnp.asarray(frequencies())
    vmem = pl.BlockSpec(memory_space=pltpu.VMEM)
    anywhere = pl.BlockSpec(memory_space=pl.ANY)
    dma = pltpu.SemaphoreType.DMA
    hidden_out, latents_out = pl.pallas_call(
        functools.partial(kernel, group),
        name="step",
        out_shape=(
            pltpu.VMEM((1, ROWS, part), BF16),
            pltpu.VMEM((PIECE, ROWS), F32),
        ),
        in_specs=[anywhere] * 18,
        out_specs=(vmem, vmem),
        scratch_shapes=[
            pltpu.SMEM((NX * NZ * NY,), jnp.int32),
            pltpu.SMEM((1, 1), jnp.int32),
            pltpu.SMEM((alphas.shape[0],), F32),
            pltpu.VMEM((1, PAIR), F32),
            pltpu.VMEM((HEAD,), F32),
            pltpu.VMEM((HEAD,), F32),
            pltpu.VMEM((ROWS, width), BF16),
            pltpu.VMEM((ROWS, width), BF16),
            pltpu.VMEM((ROWS, part), BF16),
            pltpu.VMEM((TXT, width), BF16),
            pltpu.VMEM((TXT, width), BF16),
            pltpu.VMEM((group, width, part), BF16),
            pltpu.VMEM((part,), F32),
            pltpu.VMEM((part,), F32),
            pltpu.VMEM((part,), F32),
            pltpu.VMEM((total * PIECE, part), F32),
            pltpu.VMEM((PIECE, ROWS), F32),
            pltpu.VMEM((NZ, ROWS, width), BF16),
            pltpu.VMEM((n_kv, ROWS, width), BF16),
            pltpu.VMEM((n_kv, ROWS, width), BF16),
            pltpu.VMEM((width // PAIR, NZ, ROWS, PAIR), BF16),
            pltpu.VMEM((width // PAIR, NZ, ROWS, PAIR), BF16),
            pltpu.VMEM((NZ, 8, LANES), F32),
            pltpu.VMEM((NZ, 8, LANES), F32),
            pltpu.VMEM((max(group - 1, 1), ROWS, part), BF16),
            pltpu.VMEM((group, ROWS, part), BF16),
            pltpu.VMEM((total, 8, LANES), F32),
            pltpu.VMEM((total, 8, LANES), F32),
            dma((18,)),
            dma((7,)),
            dma((9,)),
        ],
        compiler_params=pltpu.CompilerParams(collective_id=0, has_side_effects=True),
    )(
        lengths,
        step_index.reshape(1, 1),
        alphas,
        freq,
        q_gain,
        k_gain,
        stream,
        queries,
        keys,
        values,
        text_keys,
        text_values,
        out_weight,
        gate,
        shift,
        scale,
        proj_weight.T,
        latents.T,
    )
    return finish(hidden_out, latents_out)


def solution(mesh):
    return jax.shard_map(
        functools.partial(shards, mesh.shape["tp"]),
        mesh=mesh,
        in_specs=(
            P("cfg", "seq", "tp"),
            P("cfg", "seq", "tp"),
            P("cfg", "seq", "tp"),
            P("cfg", "seq", "tp"),
            P("cfg", None, "tp"),
            P("cfg", None, "tp"),
            P("tp", None),
            P("tp"),
            P("tp"),
            P("tp"),
            P("tp", None),
            P(),
            P(),
            P(),
            P("seq", ("cfg", "tp")),
            P(),
            P(),
        ),
        out_specs=(P("cfg", "seq", "tp"), P("seq", ("cfg", "tp"))),
        check_vma=False,
    )
```

```python
import functools

import jax
import jax.numpy as jnp
import numpy as np
from jax import lax
from jax.experimental import pallas as pl
from jax.experimental.pallas import tpu as pltpu
from jax.sharding import PartitionSpec as P

NX = 4
NZ = 8
NY = 2
D = 3072
HEAD = 64
HP = 30
WP = 45
STRIDE = 20
ROWS = 40
TXT = 226
LANES = 128
PAIR = 2 * HEAD
PIECE = 8
STATS = 16

guide_scale = 6.0
head_eps = 1e-06
final_eps = 1e-05
LOW = -1e30
NEAR, PART, LAST, QUERY, OTHER, FAR, STAT, OUT = 0, 1, 2, 3, 6, 9, 12, 15
MESH = pl.DeviceIdType.MESH
F32 = jnp.float32
BF16 = jnp.bfloat16


def frequencies():
    def one(extent):
        return 1.0 / 10000.0 ** (np.arange(0, extent, 2, dtype=np.float32) / np.float32(extent))

    freq = np.concatenate([one(16), one(24), one(24)]).astype(np.float32)
    return np.repeat(freq, 2)[None, :].repeat(2, axis=0).reshape(1, PAIR)


def nt(left, right, precision=None):
    return lax.dot_general(
        left, right, (((1,), (1,)), ((), ())), precision=precision, preferred_element_type=F32
    )


def nn(left, right, precision=None):
    return lax.dot_general(
        left, right, (((1,), (0,)), ((), ())), precision=precision, preferred_element_type=F32
    )


def kernel(
    group,
    lengths_hbm,
    step_index_hbm,
    alphas_hbm,
    freq_hbm,
    q_gain_hbm,
    k_gain_hbm,
    stream_hbm,
    queries_hbm,
    keys_hbm,
    values_hbm,
    text_keys_hbm,
    text_values_hbm,
    weight_hbm,
    gate_hbm,
    shift_hbm,
    scale_hbm,
    proj_hbm,
    latents_hbm,
    hidden_out,
    latents_out,
    lengths,
    step_index,
    alphas,
    freq,
    q_gain,
    k_gain,
    queries,
    keys,
    stream,
    text_keys,
    text_values,
    weight,
    gate,
    shift,
    scale,
    proj,
    latents,
    qbuf,
    kbuf,
    vbuf,
    osend,
    obuf,
    ssend,
    sbuf,
    sjoin,
    acc,
    rsend,
    rbuf,
    fsend,
    fbuf,
    load_sem,
    send_sem,
    recv_sem,
):
    n_kv = NX * NY
    total = 2 * group
    width = queries.shape[1]
    pairs = width // PAIR
    part = width * 2
    c = lax.axis_index("cfg")
    s = lax.axis_index("seq")
    t = lax.axis_index("tp")
    y = lax.rem(s, NY)
    z = lax.rem(lax.div(s, NY), NZ)
    x = lax.div(s, NY * NZ)
    rank = c * group + t

    def place(xx, zz, yy):
        return (c, (xx * NZ + zz) * NY + yy, t)

    z_of = [lax.rem(z + d, NZ) for d in range(1, NZ)]
    z_peers = [place(x, zz, y) for zz in z_of]
    x_of = [lax.rem(x + d, NX) for d in range(1, NX)]
    x_peers = [place(xx, z, y) for xx in x_of]
    y_peer = place(x, z, 1 - y)
    t_of = [t + 1 - 2 * lax.rem(t, 2), lax.rem(t + 2, group), group - 1 - t][: group - 1]
    t_peers = [(c, s, tt) for tt in t_of]
    g_of = [lax.rem(rank + d, total) for d in range(1, total)]
    g_peers = [(lax.div(g, group), s, lax.rem(g, group)) for g in g_of]

    barrier = pltpu.get_barrier_semaphore()
    everyone = z_peers + x_peers + ([y_peer] if NY > 1 else []) + g_peers
    for peer in everyone:
        pl.semaphore_signal(barrier, inc=1, device_id=peer, device_id_type=MESH)

    own = x * NY + y
    other = x * NY + (1 - y)

    def load(src, dst, which):
        copy = pltpu.make_async_copy(src, dst, load_sem.at[which])
        copy.start()
        return copy

    load_small = [
        load(lengths_hbm, lengths, 0),
        load(freq_hbm, freq, 1),
        load(q_gain_hbm, q_gain, 2),
        load(k_gain_hbm, k_gain, 3),
    ]
    load_k = load(keys_hbm.at[0], keys, 4)
    load_q = load(queries_hbm.at[0], queries, 5)
    for p in range(pairs):
        load(values_hbm.at[0, :, pl.ds(p * PAIR, PAIR)], vbuf.at[p, own], 6)
    load_text = [load(text_keys_hbm.at[0], text_keys, 7), load(text_values_hbm.at[0], text_values, 8)]
    for j in range(group):
        load(weight_hbm.at[:, pl.ds(j * part, part)], weight.at[j], 9)
    load_rest = [
        load(step_index_hbm, step_index, 10),
        load(alphas_hbm, alphas, 11),
        load(stream_hbm.at[0], stream, 12),
        load(gate_hbm, gate, 13),
        load(shift_hbm, shift, 14),
        load(scale_hbm, scale, 15),
        load(proj_hbm, proj, 16),
        load(latents_hbm, latents, 17),
    ]

    for copy in load_small:
        copy.wait()
    lane = lax.broadcasted_iota(jnp.int32, (1, PAIR), 1)
    within_head = lax.rem(lane, HEAD)
    is_even = lax.rem(lane, 2) == 0
    first_head = lane < HEAD
    own_start = jnp.int32(0)
    for b in range(NX * NZ * NY):
        own_start = own_start + jnp.where(b < s, lengths[b], 0)
    own_count = lengths[s]
    row = lax.broadcasted_iota(jnp.int32, (ROWS, PAIR), 0)
    live_rows = row < own_count
    position = (row + own_start).astype(F32)
    frame = jnp.floor((position + 0.5) * (1.0 / (HP * WP)))
    line = jnp.floor((position + 0.5) * (1.0 / WP))
    across = position - line * WP
    height = line - frame * HP
    coord = jnp.where(within_head < 16, frame, jnp.where(within_head < 40, height, across))
    angle = coord * freq[...]
    cos_table = jnp.cos(angle)
    sin_table = jnp.sin(angle)
    sin_table = jnp.where(is_even, -sin_table, sin_table)

    r_io = lax.broadcasted_iota(jnp.int32, (PAIR, PAIR), 0)
    c_io = lax.broadcasted_iota(jnp.int32, (PAIR, PAIR), 1)
    mean_matrix = jnp.where((r_io < HEAD) == (c_io < HEAD), 1.0 / HEAD, 0.0)
    mean_matrix_low = mean_matrix.astype(BF16)
    gain_q = q_gain[...].reshape(1, HEAD)
    gain_q = jnp.concatenate([gain_q, gain_q], axis=1)
    gain_k = k_gain[...].reshape(1, HEAD)
    gain_k = jnp.concatenate([gain_k, gain_k], axis=1)

    def head_norm(field, gain):
        centre = field.astype(F32) - nn(field, mean_matrix_low)
        square = centre * centre
        high = square.astype(BF16)
        low = (square - high.astype(F32)).astype(BF16)
        spread = nn(high, mean_matrix_low) + nn(low, mean_matrix_low)
        return centre * lax.rsqrt(spread + head_eps) * gain

    def rotate(field):
        swapped = jnp.where(
            is_even, pltpu.roll(field, PAIR - 1, 1), pltpu.roll(field, 1, 1)
        )
        return field * cos_table + swapped * sin_table

    def pair_slice(p):
        return pl.ds(p * PAIR, PAIR)

    load_k.wait()
    for p in range(pairs):
        made = rotate(head_norm(keys[:, pair_slice(p)], gain_k)).astype(BF16)
        kbuf[p, own] = made
    pl.semaphore_wait(barrier, len(everyone))

    def send(src, dst, kind, which, peer):
        copy = pltpu.make_async_remote_copy(
            src_ref=src,
            dst_ref=dst,
            send_sem=send_sem.at[kind],
            recv_sem=recv_sem.at[which],
            device_id=peer,
            device_id_type=MESH,
        )
        copy.start()

    def whole_copy(ref, kind, which):
        return pltpu.make_async_remote_copy(
            src_ref=ref,
            dst_ref=ref,
            send_sem=send_sem.at[kind],
            recv_sem=recv_sem.at[which],
            device_id=g_peers[0],
            device_id_type=MESH,
        )

    def arrive(ref, which):
        whole_copy(ref, 0, which).wait_recv()

    for p in range(pairs):
        if NY > 1:
            for to in (y_peer,):
                send(kbuf.at[p, own], kbuf.at[p, own], 0, OTHER + p, to)
                send(values_hbm.at[0, :, pair_slice(p)], vbuf.at[p, own], 1, OTHER + p, to)
    for p in range(pairs):
        for to in x_peers:
            send(kbuf.at[p, own], kbuf.at[p, own], 0, NEAR, to)
            send(values_hbm.at[0, :, pair_slice(p)], vbuf.at[p, own], 1, NEAR, to)

    order_z = sorted(range(1, NZ), key=lambda d: -min(d, NZ - d))
    load_q.wait()
    for p in range(pairs):
        made = rotate(head_norm(queries[:, pair_slice(p)], gain_q)).astype(BF16)
        qbuf[p, z] = made
        for d in order_z:
            send(qbuf.at[p, z], qbuf.at[p, z], 2, QUERY + p, z_peers[d - 1])

    for copy in load_text:
        copy.wait()
    text_mixed = []
    lane_row = lax.broadcasted_iota(jnp.int32, (ROWS, LANES), 1)
    text_stat = jnp.where(lax.rem(lane_row, 8) >= 6, 1.0, 0.0)
    for p in range(pairs):
        made = head_norm(text_keys[:, pair_slice(p)], gain_k)
        query_part = qbuf[p, z]
        value_part = text_values[:, pair_slice(p)]
        outs = []
        for which in range(2):
            chosen = first_head if which == 0 else jnp.logical_not(first_head)
            key_part = jnp.where(chosen, made, 0.0).astype(BF16)
            scores = nt(query_part, key_part) * 0.125
            top = jnp.max(scores, axis=1, keepdims=True)
            weights = jnp.exp(scores - top)
            count = jnp.sum(weights, axis=1, keepdims=True)
            outs.append(nn(weights.astype(BF16), value_part))
            head = 2 * p + which
            text_stat = jnp.where(lane_row == head, top, text_stat)
            text_stat = jnp.where(lane_row == 8 + head, count, text_stat)
        text_mixed.append(jnp.where(first_head, outs[0], outs[1]))
    below = jnp.zeros((LANES - ROWS, LANES), F32)
    text_stat = jnp.concatenate([text_stat, below], axis=0).T
    lane_tile = lax.broadcasted_iota(jnp.int32, (8, LANES), 1)
    text_stat = jnp.where(
        lane_tile < HEAD, text_stat[0:8], pltpu.roll(text_stat[8:16], HEAD, 1)
    )

    for p in range(pairs):
        if NY > 1:
            arrive(kbuf.at[p, pl.ds(0, 2)], OTHER + p)
            for to in x_peers:
                send(kbuf.at[p, other], kbuf.at[p, other], 0, FAR + p, to)
                send(vbuf.at[p, other], vbuf.at[p, other], 1, FAR + p, to)
    arrive(kbuf.at[:, pl.ds(0, 2 * (NX - 1))], NEAR)
    pltpu.make_async_copy(vbuf.at[:, 0], vbuf.at[:, 0], load_sem.at[6]).wait()

    n_keys = NX * ROWS
    n_queries = NZ * ROWS
    q_up = -(-n_queries // LANES) * LANES
    slot_row = lax.broadcasted_iota(jnp.int32, (ROWS, 1), 0)

    def gather(buf, p, yy):
        blocks = [buf[p, j * NY + yy].astype(F32) for j in range(NX)]
        return jnp.concatenate(blocks, axis=0)

    def live_of(yy):
        pieces = [
            jnp.where(slot_row < lengths[(j * NZ + z) * NY + yy], 0.0, LOW) for j in range(NX)
        ]
        return jnp.concatenate(pieces + pieces, axis=0)

    def score(p, yy, live):
        key_part = gather(kbuf, p, yy)
        both = jnp.concatenate(
            [jnp.where(first_head, key_part, 0.0), jnp.where(first_head, 0.0, key_part)], axis=0
        ).astype(BF16)
        found = jnp.where(live < 0.0, LOW, nt(both, query_parts[p]) * 0.125)
        turned = gather(vbuf, p, yy).T.astype(BF16)
        return [
            (found[w * n_keys : (w + 1) * n_keys], turned[w * HEAD : (w + 1) * HEAD])
            for w in range(2)
        ]

    query_parts = []
    partials = []
    live = live_of(y)
    for p in range(pairs):
        arrive(qbuf.at[p, pl.ds(0, NZ - 1)], QUERY + p)
        query_parts.append(
            jnp.concatenate([qbuf[p, j].astype(F32) for j in range(NZ)], axis=0).astype(BF16)
        )
        for scores, turned in score(p, y, live):
            top = jnp.max(scores, axis=0, keepdims=True)
            weights = jnp.exp(scores - top)
            count = jnp.sum(weights, axis=0, keepdims=True)
            partials.append((top, count, nn(turned, weights.astype(BF16))))

    live = live_of(1 - y)
    stat_row = lax.broadcasted_iota(jnp.int32, (8, q_up), 0)

    def widen(line):
        if q_up == n_queries:
            return line
        return jnp.concatenate([line, jnp.zeros((line.shape[0], q_up - n_queries), F32)], axis=1)

    for p in range(pairs):
        outs = []
        if NY > 1:
            arrive(kbuf.at[p, pl.ds(0, 2 * (NX - 1))], FAR + p)
            far = score(p, 1 - y, live)
        for which in range(2):
            head = 2 * p + which
            top, count, out = partials[head]
            if NY > 1:
                scores, turned = far[which]
                before = top
                top = jnp.maximum(before, jnp.max(scores, axis=0, keepdims=True))
                fade = jnp.exp(before - top)
                weights = jnp.exp(scores - top)
                count = count * fade + jnp.sum(weights, axis=0, keepdims=True)
                out = out * fade + nn(turned, weights.astype(BF16))
            outs.append(out)
            tops = widen(top) if which == 0 else jnp.where(stat_row == 0, tops, widen(top))
            counts = widen(count) if which == 0 else jnp.where(stat_row == 0, counts, widen(count))
        mixed = widen(jnp.concatenate(outs, axis=0)).T
        for j in range(NZ):
            osend[p, j] = mixed[j * ROWS : (j + 1) * ROWS].astype(BF16)
        for j in range(NZ):
            left = pltpu.roll(tops, (q_up - j * ROWS) % q_up, 1)[:, 0:LANES]
            right = pltpu.roll(counts, (q_up + HEAD - j * ROWS) % q_up, 1)[:, 0:LANES]
            ssend[p, j] = jnp.where(lane_tile < HEAD, left, right)[0:2]
        for d in order_z:
            zz = z_of[d - 1]
            send(ssend.at[p, zz], sbuf.at[p, z], 3, STAT + p, z_peers[d - 1])
            send(osend.at[p, zz], obuf.at[p, z], 4, OUT + p, z_peers[d - 1])

    pltpu.make_async_copy(weight, weight, load_sem.at[9]).wait()
    for w in range(2):
        sjoin[w] = jnp.where(lax.broadcasted_iota(jnp.int32, (16, LANES), 1) < HEAD, LOW, 0.0)
    for p in range(pairs):
        arrive(sbuf.at[p, pl.ds(0, NZ - 1)], STAT + p)
        arrive(obuf.at[p, pl.ds(0, NZ - 1)], OUT + p)
        stats = [ssend[p, z]] + [sbuf[p, zz] for zz in z_of] + [text_stat[2 * p : 2 * p + 2]]
        for w in range(2):
            for j, one in enumerate(stats):
                sjoin[w, j : j + 1, :] = one[w : w + 1]
        shares = []
        for w in range(2):
            found = sjoin[w]
            count = pltpu.roll(found, HEAD, 1)
            factor = jnp.exp(found - jnp.max(found, axis=0, keepdims=True))
            shares.append(factor / jnp.sum(factor * count, axis=0, keepdims=True))
        share = jnp.concatenate(shares + [jnp.zeros((LANES - 32, LANES), F32)], axis=0).T
        pieces = [osend[p, z]] + [obuf[p, zz] for zz in z_of]
        pieces = [piece.astype(F32) for piece in pieces] + [text_mixed[p]]
        joined = jnp.zeros((ROWS, PAIR), F32)
        for j, piece in enumerate(pieces):
            lower = share[0:ROWS, j : j + 1]
            upper = share[0:ROWS, 16 + j : 17 + j]
            joined = joined + piece * jnp.where(first_head, lower, upper)
        attended = joined.astype(BF16)
        if p < pairs - 1:
            for j in range(group):
                more = nn(attended, weight[j, pair_slice(p), :])
                acc[j] = more if p == 0 else acc[j] + more
    for d in range(1, group):
        tt = t_of[d - 1]
        rsend[d - 1] = (acc[tt] + nn(attended, weight[tt, pair_slice(pairs - 1), :])).astype(BF16)
        send(rsend.at[d - 1], rbuf.at[t], 5, PART, t_peers[d - 1])
    summed = acc[t] + nn(attended, weight[t, pair_slice(pairs - 1), :])
    for copy in load_rest:
        copy.wait()
    lifted = 1.0 + scale[...].reshape(1, part)
    arrive(rbuf.at[pl.ds(0, group - 1)], PART)
    for tt in t_of:
        summed = summed + rbuf[tt].astype(F32)
    hidden = stream[...].astype(F32) + gate[...].reshape(1, part) * summed
    hidden = jnp.where(live_rows[:, 0:1], hidden, 0.0).astype(BF16)
    hidden_out[0] = hidden
    widened = hidden.astype(F32)

    channels = total * PIECE
    tall = ROWS + 8
    extra = jnp.concatenate([lifted, shift[...].reshape(1, part), jnp.zeros((6, part), F32)], axis=0)
    stacked = jnp.concatenate([widened * lifted, extra], axis=0)
    flipped = nt(proj[...], stacked, lax.Precision.HIGHEST)
    row_sum = nt(jnp.ones((8, part), BF16), hidden)
    row_square = nt(jnp.ones((8, part), F32), widened * widened, lax.Precision.HIGHEST)
    flipped = jnp.concatenate([flipped, jnp.zeros((channels, HEAD - tall), F32)], axis=1)
    sums = jnp.where(lax.broadcasted_iota(jnp.int32, (8, ROWS), 0) == 0, row_sum, row_square)
    sums = jnp.concatenate([sums, jnp.zeros((8, HEAD - ROWS), F32)], axis=1)
    for g in range(total):
        fsend[g] = jnp.concatenate([flipped[g * PIECE : (g + 1) * PIECE], sums], axis=1)
    for d in range(1, total):
        g = g_of[d - 1]
        send(fsend.at[g], fbuf.at[rank], 6, LAST, g_peers[d - 1])
    arrive(fbuf.at[pl.ds(0, total - 1)], LAST)

    def prediction(half):
        gathered = jnp.zeros((8, LANES), F32)
        for tt in range(group):
            g = half * group + tt
            gathered = gathered + jnp.where(rank == g, fsend[g], fbuf[g])
        sums = pltpu.roll(gathered, HEAD, 1)
        mean = sums[0:1] / D
        square = sums[1:2] / D
        base = gathered
        ratio = lax.rsqrt(square - mean * mean + final_eps)
        lifted_sum = base[:, ROWS : ROWS + 1]
        shift_sum = base[:, ROWS + 1 : ROWS + 2]
        return ratio * (base - mean * lifted_sum) + shift_sum

    conditioned = prediction(0)
    unconditioned = prediction(1)
    guided = unconditioned + guide_scale * (conditioned - unconditioned)
    guided = guided[:, 0:ROWS]
    step = step_index[0, 0]
    current = jnp.zeros((1, ROWS), F32) + alphas[step]
    earlier = jnp.zeros((1, ROWS), F32) + alphas[jnp.maximum(step - STRIDE, 0)]
    root_now = jnp.sqrt(current)
    rest_now = jnp.sqrt(1.0 - current)
    held = latents[...]
    clean = root_now * held - rest_now * guided
    noise = root_now * guided + rest_now * held
    stepped = jnp.sqrt(earlier) * clean + jnp.sqrt(1.0 - earlier) * noise
    token = lax.broadcasted_iota(jnp.int32, (1, ROWS), 1)
    latents_out[...] = jnp.where(token < own_count, stepped, 0.0)

    n_block = NX - 1 + (NX if NY > 1 else 0)
    for kind, ref in enumerate(
        [
            kbuf.at[:, pl.ds(0, n_block)],
            vbuf.at[:, pl.ds(0, n_block)],
            qbuf.at[:, pl.ds(0, NZ - 1)],
            sbuf.at[:, pl.ds(0, NZ - 1)],
            obuf.at[:, pl.ds(0, NZ - 1)],
            rbuf.at[pl.ds(0, group - 1)],
            fbuf.at[pl.ds(0, total - 1)],
        ]
    ):
        whole_copy(ref, kind, 0).wait_send()


def finish_kernel(hidden, latents, hidden_out, latents_out, sem):
    copies = [
        pltpu.make_async_copy(hidden, hidden_out, sem.at[0]),
        pltpu.make_async_copy(latents, latents_out, sem.at[1]),
    ]
    for copy in copies:
        copy.start()
    for copy in copies:
        copy.wait()


def finish(hidden, latents):
    vmem = pl.BlockSpec(memory_space=pltpu.VMEM)
    anywhere = pl.BlockSpec(memory_space=pl.ANY)
    hidden, latents = pl.pallas_call(
        finish_kernel,
        name="finish",
        out_shape=(
            jax.ShapeDtypeStruct(hidden.shape, hidden.dtype),
            jax.ShapeDtypeStruct(latents.shape, latents.dtype),
        ),
        in_specs=[vmem, vmem],
        out_specs=(anywhere, anywhere),
        scratch_shapes=[pltpu.SemaphoreType.DMA((2,))],
    )(
        pltpu.with_memory_space_constraint(hidden, pltpu.VMEM),
        pltpu.with_memory_space_constraint(latents, pltpu.VMEM),
    )
    return hidden, latents.T


def shards(
    group,
    stream,
    queries,
    keys,
    values,
    text_keys,
    text_values,
    out_weight,
    gate,
    shift,
    scale,
    proj_weight,
    q_gain,
    k_gain,
    lengths,
    latents,
    alphas,
    step_index,
):
    width = queries.shape[2]
    part = stream.shape[2]
    n_kv = NX * NY
    total = 2 * group
    freq = jnp.asarray(frequencies())
    vmem = pl.BlockSpec(memory_space=pltpu.VMEM)
    anywhere = pl.BlockSpec(memory_space=pl.ANY)
    dma = pltpu.SemaphoreType.DMA
    hidden_out, latents_out = pl.pallas_call(
        functools.partial(kernel, group),
        name="step",
        out_shape=(
            pltpu.VMEM((1, ROWS, part), BF16),
            pltpu.VMEM((PIECE, ROWS), F32),
        ),
        in_specs=[anywhere] * 18,
        out_specs=(vmem, vmem),
        scratch_shapes=[
            pltpu.SMEM((NX * NZ * NY,), jnp.int32),
            pltpu.SMEM((1, 1), jnp.int32),
            pltpu.SMEM((alphas.shape[0],), F32),
            pltpu.VMEM((1, PAIR), F32),
            pltpu.VMEM((HEAD,), F32),
            pltpu.VMEM((HEAD,), F32),
            pltpu.VMEM((ROWS, width), BF16),
            pltpu.VMEM((ROWS, width), BF16),
            pltpu.VMEM((ROWS, part), BF16),
            pltpu.VMEM((TXT, width), BF16),
            pltpu.VMEM((TXT, width), BF16),
            pltpu.VMEM((group, width, part), BF16),
            pltpu.VMEM((part,), F32),
            pltpu.VMEM((part,), F32),
            pltpu.VMEM((part,), F32),
            pltpu.VMEM((total * PIECE, part), F32),
            pltpu.VMEM((PIECE, ROWS), F32),
            pltpu.VMEM((width // PAIR, NZ, ROWS, PAIR), BF16),
            pltpu.VMEM((width // PAIR, n_kv, ROWS, PAIR), BF16),
            pltpu.VMEM((width // PAIR, n_kv, ROWS, PAIR), BF16),
            pltpu.VMEM((width // PAIR, NZ, ROWS, PAIR), BF16),
            pltpu.VMEM((width // PAIR, NZ, ROWS, PAIR), BF16),
            pltpu.VMEM((width // PAIR, NZ, 2, LANES), F32),
            pltpu.VMEM((width // PAIR, NZ, 2, LANES), F32),
            pltpu.VMEM((2, 16, LANES), F32),
            pltpu.VMEM((group, ROWS, part), F32),
            pltpu.VMEM((max(group - 1, 1), ROWS, part), BF16),
            pltpu.VMEM((group, ROWS, part), BF16),
            pltpu.VMEM((total, 8, LANES), F32),
            pltpu.VMEM((total, 8, LANES), F32),
            dma((18,)),
            dma((7,)),
            dma((18,)),
        ],
        compiler_params=pltpu.CompilerParams(collective_id=0, has_side_effects=True),
    )(
        lengths,
        step_index.reshape(1, 1),
        alphas,
        freq,
        q_gain,
        k_gain,
        stream,
        queries,
        keys,
        values,
        text_keys,
        text_values,
        out_weight,
        gate,
        shift,
        scale,
        proj_weight.T,
        latents.T,
    )
    return finish(hidden_out, latents_out)


def solution(mesh):
    return jax.shard_map(
        functools.partial(shards, mesh.shape["tp"]),
        mesh=mesh,
        in_specs=(
            P("cfg", "seq", "tp"),
            P("cfg", "seq", "tp"),
            P("cfg", "seq", "tp"),
            P("cfg", "seq", "tp"),
            P("cfg", None, "tp"),
            P("cfg", None, "tp"),
            P("tp", None),
            P("tp"),
            P("tp"),
            P("tp"),
            P("tp", None),
            P(),
            P(),
            P(),
            P("seq", ("cfg", "tp")),
            P(),
            P(),
        ),
        out_specs=(P("cfg", "seq", "tp"), P("seq", ("cfg", "tp"))),
        check_vma=False,
    )
```

```python
import functools

import jax
import jax.numpy as jnp
import numpy as np
from jax import lax
from jax.experimental import pallas as pl
from jax.experimental.pallas import tpu as pltpu
from jax.sharding import PartitionSpec as P

NX = 4
NZ = 8
NY = 2
D = 3072
HEAD = 64
HP = 30
WP = 45
STRIDE = 20
ROWS = 40
TXT = 226
LANES = 128
PAIR = 2 * HEAD
PIECE = 8
STATS = 16

guide_scale = 6.0
head_eps = 1e-06
final_eps = 1e-05
LOW = -1e30
NEAR, PART, LAST, QUERY, OTHER, FAR, STAT, OUT = 0, 1, 2, 3, 6, 9, 12, 15
MESH = pl.DeviceIdType.MESH
F32 = jnp.float32
BF16 = jnp.bfloat16


def frequencies():
    def one(extent):
        return 1.0 / 10000.0 ** (np.arange(0, extent, 2, dtype=np.float32) / np.float32(extent))

    freq = np.concatenate([one(16), one(24), one(24)]).astype(np.float32)
    return np.repeat(freq, 2)[None, :].repeat(2, axis=0).reshape(1, PAIR)


def nt(left, right, precision=None):
    return lax.dot_general(
        left, right, (((1,), (1,)), ((), ())), precision=precision, preferred_element_type=F32
    )


def nn(left, right, precision=None):
    return lax.dot_general(
        left, right, (((1,), (0,)), ((), ())), precision=precision, preferred_element_type=F32
    )


def kernel(
    group,
    lengths_hbm,
    step_index_hbm,
    alphas_hbm,
    freq_hbm,
    q_gain_hbm,
    k_gain_hbm,
    stream_hbm,
    queries_hbm,
    keys_hbm,
    values_hbm,
    text_keys_hbm,
    text_values_hbm,
    weight_hbm,
    gate_hbm,
    shift_hbm,
    scale_hbm,
    proj_hbm,
    latents_hbm,
    hidden_out,
    latents_out,
    lengths,
    step_index,
    alphas,
    freq,
    q_gain,
    k_gain,
    queries,
    keys,
    stream,
    text_keys,
    text_values,
    weight,
    gate,
    shift,
    scale,
    proj,
    latents,
    qbuf,
    kbuf,
    vbuf,
    osend,
    obuf,
    ssend,
    sbuf,
    sjoin,
    acc,
    rsend,
    rbuf,
    fsend,
    fbuf,
    load_sem,
    send_sem,
    recv_sem,
):
    n_kv = NX * NY
    total = 2 * group
    width = queries.shape[1]
    pairs = width // PAIR
    part = width * 2
    c = lax.axis_index("cfg")
    s = lax.axis_index("seq")
    t = lax.axis_index("tp")
    y = lax.rem(s, NY)
    z = lax.rem(lax.div(s, NY), NZ)
    x = lax.div(s, NY * NZ)
    rank = c * group + t

    def place(xx, zz, yy):
        return (c, (xx * NZ + zz) * NY + yy, t)

    z_of = [lax.rem(z + d, NZ) for d in range(1, NZ)]
    z_peers = [place(x, zz, y) for zz in z_of]
    x_of = [lax.rem(x + d, NX) for d in range(1, NX)]
    x_peers = [place(xx, z, y) for xx in x_of]
    y_peer = place(x, z, 1 - y)
    t_of = [t + 1 - 2 * lax.rem(t, 2), lax.rem(t + 2, group), group - 1 - t][: group - 1]
    t_peers = [(c, s, tt) for tt in t_of]
    g_of = [lax.rem(rank + d, total) for d in range(1, total)]
    g_peers = [(lax.div(g, group), s, lax.rem(g, group)) for g in g_of]

    barrier = pltpu.get_barrier_semaphore()
    everyone = z_peers + x_peers + ([y_peer] if NY > 1 else []) + g_peers
    for peer in everyone:
        pl.semaphore_signal(barrier, inc=1, device_id=peer, device_id_type=MESH)

    own = x * NY + y
    other = x * NY + (1 - y)

    def load(src, dst, which):
        copy = pltpu.make_async_copy(src, dst, load_sem.at[which])
        copy.start()
        return copy

    load_small = [
        load(lengths_hbm, lengths, 0),
        load(freq_hbm, freq, 1),
        load(q_gain_hbm, q_gain, 2),
        load(k_gain_hbm, k_gain, 3),
    ]
    load_k = load(keys_hbm.at[0], keys, 4)
    load_q = load(queries_hbm.at[0], queries, 5)
    for p in range(pairs):
        load(values_hbm.at[0, :, pl.ds(p * PAIR, PAIR)], vbuf.at[p, own], 6)
    load_text = [load(text_keys_hbm.at[0], text_keys, 7), load(text_values_hbm.at[0], text_values, 8)]
    for j in range(group):
        load(weight_hbm.at[:, pl.ds(j * part, part)], weight.at[j], 9)
    load_rest = [
        load(step_index_hbm, step_index, 10),
        load(alphas_hbm, alphas, 11),
        load(stream_hbm.at[0], stream, 12),
        load(gate_hbm, gate, 13),
        load(shift_hbm, shift, 14),
        load(scale_hbm, scale, 15),
        load(proj_hbm, proj, 16),
        load(latents_hbm, latents, 17),
    ]

    for copy in load_small:
        copy.wait()
    lane = lax.broadcasted_iota(jnp.int32, (1, PAIR), 1)
    within_head = lax.rem(lane, HEAD)
    is_even = lax.rem(lane, 2) == 0
    first_head = lane < HEAD
    own_start = jnp.int32(0)
    for b in range(NX * NZ * NY):
        own_start = own_start + jnp.where(b < s, lengths[b], 0)
    own_count = lengths[s]
    row = lax.broadcasted_iota(jnp.int32, (ROWS, PAIR), 0)
    live_rows = row < own_count
    position = (row + own_start).astype(F32)
    frame = jnp.floor((position + 0.5) * (1.0 / (HP * WP)))
    line = jnp.floor((position + 0.5) * (1.0 / WP))
    across = position - line * WP
    height = line - frame * HP
    coord = jnp.where(within_head < 16, frame, jnp.where(within_head < 40, height, across))
    angle = coord * freq[...]
    cos_table = jnp.cos(angle)
    sin_table = jnp.sin(angle)
    sin_table = jnp.where(is_even, -sin_table, sin_table)

    r_io = lax.broadcasted_iota(jnp.int32, (PAIR, PAIR), 0)
    c_io = lax.broadcasted_iota(jnp.int32, (PAIR, PAIR), 1)
    mean_matrix = jnp.where((r_io < HEAD) == (c_io < HEAD), 1.0 / HEAD, 0.0)
    mean_matrix_low = mean_matrix.astype(BF16)
    gain_q = q_gain[...].reshape(1, HEAD)
    gain_q = jnp.concatenate([gain_q, gain_q], axis=1)
    gain_k = k_gain[...].reshape(1, HEAD)
    gain_k = jnp.concatenate([gain_k, gain_k], axis=1)

    def head_norm(field, gain):
        centre = field.astype(F32) - nn(field, mean_matrix_low)
        square = centre * centre
        high = square.astype(BF16)
        low = (square - high.astype(F32)).astype(BF16)
        spread = nn(high, mean_matrix_low) + nn(low, mean_matrix_low)
        return centre * lax.rsqrt(spread + head_eps) * gain

    def rotate(field):
        swapped = jnp.where(
            is_even, pltpu.roll(field, PAIR - 1, 1), pltpu.roll(field, 1, 1)
        )
        return field * cos_table + swapped * sin_table

    def pair_slice(p):
        return pl.ds(p * PAIR, PAIR)

    load_k.wait()
    for p in range(pairs):
        made = rotate(head_norm(keys[:, pair_slice(p)], gain_k)).astype(BF16)
        kbuf[p, own] = made
    load_q.wait()
    for p in range(pairs):
        made = rotate(head_norm(queries[:, pair_slice(p)], gain_q)).astype(BF16)
        qbuf[p, z] = made
    pl.semaphore_wait(barrier, len(everyone))

    def send(src, dst, kind, which, peer):
        copy = pltpu.make_async_remote_copy(
            src_ref=src,
            dst_ref=dst,
            send_sem=send_sem.at[kind],
            recv_sem=recv_sem.at[which],
            device_id=peer,
            device_id_type=MESH,
        )
        copy.start()

    def whole_copy(ref, kind, which):
        return pltpu.make_async_remote_copy(
            src_ref=ref,
            dst_ref=ref,
            send_sem=send_sem.at[kind],
            recv_sem=recv_sem.at[which],
            device_id=g_peers[0],
            device_id_type=MESH,
        )

    def arrive(ref, which):
        whole_copy(ref, 0, which).wait_recv()

    for p in range(pairs):
        if NY > 1:
            for to in (y_peer,):
                send(kbuf.at[p, own], kbuf.at[p, own], 0, OTHER + p, to)
                send(values_hbm.at[0, :, pair_slice(p)], vbuf.at[p, own], 1, OTHER + p, to)
    for p in range(pairs):
        for to in x_peers:
            send(kbuf.at[p, own], kbuf.at[p, own], 0, NEAR, to)
            send(values_hbm.at[0, :, pair_slice(p)], vbuf.at[p, own], 1, NEAR, to)

    order_z = sorted(range(1, NZ), key=lambda d: -min(d, NZ - d))
    for p in range(pairs):
        for d in order_z:
            send(qbuf.at[p, z], qbuf.at[p, z], 2, QUERY + p, z_peers[d - 1])

    for copy in load_text:
        copy.wait()
    text_mixed = []
    lane_row = lax.broadcasted_iota(jnp.int32, (ROWS, LANES), 1)
    text_stat = jnp.where(lax.rem(lane_row, 8) >= 6, 1.0, 0.0)
    for p in range(pairs):
        made = head_norm(text_keys[:, pair_slice(p)], gain_k)
        query_part = qbuf[p, z]
        value_part = text_values[:, pair_slice(p)]
        outs = []
        for which in range(2):
            chosen = first_head if which == 0 else jnp.logical_not(first_head)
            key_part = jnp.where(chosen, made, 0.0).astype(BF16)
            scores = nt(query_part, key_part) * 0.125
            top = jnp.max(scores, axis=1, keepdims=True)
            weights = jnp.exp(scores - top)
            count = jnp.sum(weights, axis=1, keepdims=True)
            outs.append(nn(weights.astype(BF16), value_part))
            head = 2 * p + which
            text_stat = jnp.where(lane_row == head, top, text_stat)
            text_stat = jnp.where(lane_row == 8 + head, count, text_stat)
        text_mixed.append(jnp.where(first_head, outs[0], outs[1]))
    below = jnp.zeros((LANES - ROWS, LANES), F32)
    text_stat = jnp.concatenate([text_stat, below], axis=0).T
    lane_tile = lax.broadcasted_iota(jnp.int32, (8, LANES), 1)
    text_stat = jnp.where(
        lane_tile < HEAD, text_stat[0:8], pltpu.roll(text_stat[8:16], HEAD, 1)
    )

    for p in range(pairs):
        if NY > 1:
            arrive(kbuf.at[p, pl.ds(0, 2)], OTHER + p)
            for to in x_peers:
                send(kbuf.at[p, other], kbuf.at[p, other], 0, FAR + p, to)
                send(vbuf.at[p, other], vbuf.at[p, other], 1, FAR + p, to)
    arrive(kbuf.at[:, pl.ds(0, 2 * (NX - 1))], NEAR)
    pltpu.make_async_copy(vbuf.at[:, 0], vbuf.at[:, 0], load_sem.at[6]).wait()

    n_keys = NX * ROWS
    n_queries = NZ * ROWS
    q_up = -(-n_queries // LANES) * LANES
    slot_row = lax.broadcasted_iota(jnp.int32, (ROWS, 1), 0)

    def gather(buf, p, yy):
        blocks = [buf[p, j * NY + yy].astype(F32) for j in range(NX)]
        return jnp.concatenate(blocks, axis=0)

    def live_of(yy):
        pieces = [
            jnp.where(slot_row < lengths[(j * NZ + z) * NY + yy], 0.0, LOW) for j in range(NX)
        ]
        return jnp.concatenate(pieces + pieces, axis=0)

    def score(p, yy, live):
        key_part = gather(kbuf, p, yy)
        both = jnp.concatenate(
            [jnp.where(first_head, key_part, 0.0), jnp.where(first_head, 0.0, key_part)], axis=0
        ).astype(BF16)
        found = jnp.where(live < 0.0, LOW, nt(both, query_parts[p]) * 0.125)
        turned = gather(vbuf, p, yy).T.astype(BF16)
        return [
            (found[w * n_keys : (w + 1) * n_keys], turned[w * HEAD : (w + 1) * HEAD])
            for w in range(2)
        ]

    query_parts = []
    partials = []
    live = live_of(y)
    for p in range(pairs):
        arrive(qbuf.at[p, pl.ds(0, NZ - 1)], QUERY + p)
        query_parts.append(
            jnp.concatenate([qbuf[p, j].astype(F32) for j in range(NZ)], axis=0).astype(BF16)
        )
        for scores, turned in score(p, y, live):
            top = jnp.max(scores, axis=0, keepdims=True)
            weights = jnp.exp(scores - top)
            count = jnp.sum(weights, axis=0, keepdims=True)
            partials.append((top, count, nn(turned, weights.astype(BF16))))

    live = live_of(1 - y)
    stat_row = lax.broadcasted_iota(jnp.int32, (8, q_up), 0)

    def widen(line):
        if q_up == n_queries:
            return line
        return jnp.concatenate([line, jnp.zeros((line.shape[0], q_up - n_queries), F32)], axis=1)

    for p in range(pairs):
        outs = []
        if NY > 1:
            arrive(kbuf.at[p, pl.ds(0, 2 * (NX - 1))], FAR + p)
            far = score(p, 1 - y, live)
        for which in range(2):
            head = 2 * p + which
            top, count, out = partials[head]
            if NY > 1:
                scores, turned = far[which]
                before = top
                top = jnp.maximum(before, jnp.max(scores, axis=0, keepdims=True))
                fade = jnp.exp(before - top)
                weights = jnp.exp(scores - top)
                count = count * fade + jnp.sum(weights, axis=0, keepdims=True)
                out = out * fade + nn(turned, weights.astype(BF16))
            outs.append(out)
            tops = widen(top) if which == 0 else jnp.where(stat_row == 0, tops, widen(top))
            counts = widen(count) if which == 0 else jnp.where(stat_row == 0, counts, widen(count))
        mixed = widen(jnp.concatenate(outs, axis=0)).T
        for j in range(NZ):
            osend[p, j] = mixed[j * ROWS : (j + 1) * ROWS].astype(BF16)
        for j in range(NZ):
            left = pltpu.roll(tops, (q_up - j * ROWS) % q_up, 1)[:, 0:LANES]
            right = pltpu.roll(counts, (q_up + HEAD - j * ROWS) % q_up, 1)[:, 0:LANES]
            ssend[p, j] = jnp.where(lane_tile < HEAD, left, right)[0:2]
        for d in order_z:
            zz = z_of[d - 1]
            send(ssend.at[p, zz], sbuf.at[p, z], 3, STAT + p, z_peers[d - 1])
            send(osend.at[p, zz], obuf.at[p, z], 4, OUT + p, z_peers[d - 1])

    pltpu.make_async_copy(weight, weight, load_sem.at[9]).wait()
    for w in range(2):
        sjoin[w] = jnp.where(lax.broadcasted_iota(jnp.int32, (16, LANES), 1) < HEAD, LOW, 0.0)
    for p in range(pairs):
        arrive(sbuf.at[p, pl.ds(0, NZ - 1)], STAT + p)
        arrive(obuf.at[p, pl.ds(0, NZ - 1)], OUT + p)
        stats = [ssend[p, z]] + [sbuf[p, zz] for zz in z_of] + [text_stat[2 * p : 2 * p + 2]]
        for w in range(2):
            for j, one in enumerate(stats):
                sjoin[w, j : j + 1, :] = one[w : w + 1]
        shares = []
        for w in range(2):
            found = sjoin[w]
            count = pltpu.roll(found, HEAD, 1)
            factor = jnp.exp(found - jnp.max(found, axis=0, keepdims=True))
            shares.append(factor / jnp.sum(factor * count, axis=0, keepdims=True))
        share = jnp.concatenate(shares + [jnp.zeros((LANES - 32, LANES), F32)], axis=0).T
        pieces = [osend[p, z]] + [obuf[p, zz] for zz in z_of]
        pieces = [piece.astype(F32) for piece in pieces] + [text_mixed[p]]
        joined = jnp.zeros((ROWS, PAIR), F32)
        for j, piece in enumerate(pieces):
            lower = share[0:ROWS, j : j + 1]
            upper = share[0:ROWS, 16 + j : 17 + j]
            joined = joined + piece * jnp.where(first_head, lower, upper)
        attended = joined.astype(BF16)
        if p < pairs - 1:
            for j in range(group):
                more = nn(attended, weight[j, pair_slice(p), :])
                acc[j] = more if p == 0 else acc[j] + more
    for d in range(1, group):
        tt = t_of[d - 1]
        rsend[d - 1] = (acc[tt] + nn(attended, weight[tt, pair_slice(pairs - 1), :])).astype(BF16)
        send(rsend.at[d - 1], rbuf.at[t], 5, PART, t_peers[d - 1])
    summed = acc[t] + nn(attended, weight[t, pair_slice(pairs - 1), :])
    for copy in load_rest:
        copy.wait()
    lifted = 1.0 + scale[...].reshape(1, part)
    arrive(rbuf.at[pl.ds(0, group - 1)], PART)
    for tt in t_of:
        summed = summed + rbuf[tt].astype(F32)
    hidden = stream[...].astype(F32) + gate[...].reshape(1, part) * summed
    hidden = jnp.where(live_rows[:, 0:1], hidden, 0.0).astype(BF16)
    hidden_out[0] = hidden
    widened = hidden.astype(F32)

    channels = total * PIECE
    tall = ROWS + 8
    extra = jnp.concatenate([lifted, shift[...].reshape(1, part), jnp.zeros((6, part), F32)], axis=0)
    stacked = jnp.concatenate([widened * lifted, extra], axis=0)
    flipped = nt(proj[...], stacked, lax.Precision.HIGHEST)
    row_sum = nt(jnp.ones((8, part), BF16), hidden)
    row_square = nt(jnp.ones((8, part), F32), widened * widened, lax.Precision.HIGHEST)
    flipped = jnp.concatenate([flipped, jnp.zeros((channels, HEAD - tall), F32)], axis=1)
    sums = jnp.where(lax.broadcasted_iota(jnp.int32, (8, ROWS), 0) == 0, row_sum, row_square)
    sums = jnp.concatenate([sums, jnp.zeros((8, HEAD - ROWS), F32)], axis=1)
    for g in range(total):
        fsend[g] = jnp.concatenate([flipped[g * PIECE : (g + 1) * PIECE], sums], axis=1)
    for d in range(1, total):
        g = g_of[d - 1]
        send(fsend.at[g], fbuf.at[rank], 6, LAST, g_peers[d - 1])
    arrive(fbuf.at[pl.ds(0, total - 1)], LAST)

    def prediction(half):
        gathered = jnp.zeros((8, LANES), F32)
        for tt in range(group):
            g = half * group + tt
            gathered = gathered + jnp.where(rank == g, fsend[g], fbuf[g])
        sums = pltpu.roll(gathered, HEAD, 1)
        mean = sums[0:1] / D
        square = sums[1:2] / D
        base = gathered
        ratio = lax.rsqrt(square - mean * mean + final_eps)
        lifted_sum = base[:, ROWS : ROWS + 1]
        shift_sum = base[:, ROWS + 1 : ROWS + 2]
        return ratio * (base - mean * lifted_sum) + shift_sum

    conditioned = prediction(0)
    unconditioned = prediction(1)
    guided = unconditioned + guide_scale * (conditioned - unconditioned)
    guided = guided[:, 0:ROWS]
    step = step_index[0, 0]
    current = jnp.zeros((1, ROWS), F32) + alphas[step]
    earlier = jnp.zeros((1, ROWS), F32) + alphas[jnp.maximum(step - STRIDE, 0)]
    root_now = jnp.sqrt(current)
    rest_now = jnp.sqrt(1.0 - current)
    held = latents[...]
    clean = root_now * held - rest_now * guided
    noise = root_now * guided + rest_now * held
    stepped = jnp.sqrt(earlier) * clean + jnp.sqrt(1.0 - earlier) * noise
    token = lax.broadcasted_iota(jnp.int32, (1, ROWS), 1)
    latents_out[...] = jnp.where(token < own_count, stepped, 0.0)

    n_block = NX - 1 + (NX if NY > 1 else 0)
    for kind, ref in enumerate(
        [
            kbuf.at[:, pl.ds(0, n_block)],
            vbuf.at[:, pl.ds(0, n_block)],
            qbuf.at[:, pl.ds(0, NZ - 1)],
            sbuf.at[:, pl.ds(0, NZ - 1)],
            obuf.at[:, pl.ds(0, NZ - 1)],
            rbuf.at[pl.ds(0, group - 1)],
            fbuf.at[pl.ds(0, total - 1)],
        ]
    ):
        whole_copy(ref, kind, 0).wait_send()


def finish_kernel(hidden, latents, hidden_out, latents_out, sem):
    copies = [
        pltpu.make_async_copy(hidden, hidden_out, sem.at[0]),
        pltpu.make_async_copy(latents, latents_out, sem.at[1]),
    ]
    for copy in copies:
        copy.start()
    for copy in copies:
        copy.wait()


def finish(hidden, latents):
    vmem = pl.BlockSpec(memory_space=pltpu.VMEM)
    anywhere = pl.BlockSpec(memory_space=pl.ANY)
    hidden, latents = pl.pallas_call(
        finish_kernel,
        name="finish",
        out_shape=(
            jax.ShapeDtypeStruct(hidden.shape, hidden.dtype),
            jax.ShapeDtypeStruct(latents.shape, latents.dtype),
        ),
        in_specs=[vmem, vmem],
        out_specs=(anywhere, anywhere),
        scratch_shapes=[pltpu.SemaphoreType.DMA((2,))],
    )(
        pltpu.with_memory_space_constraint(hidden, pltpu.VMEM),
        pltpu.with_memory_space_constraint(latents, pltpu.VMEM),
    )
    return hidden, latents.T


def shards(
    group,
    stream,
    queries,
    keys,
    values,
    text_keys,
    text_values,
    out_weight,
    gate,
    shift,
    scale,
    proj_weight,
    q_gain,
    k_gain,
    lengths,
    latents,
    alphas,
    step_index,
):
    width = queries.shape[2]
    part = stream.shape[2]
    n_kv = NX * NY
    total = 2 * group
    freq = jnp.asarray(frequencies())
    vmem = pl.BlockSpec(memory_space=pltpu.VMEM)
    anywhere = pl.BlockSpec(memory_space=pl.ANY)
    dma = pltpu.SemaphoreType.DMA
    hidden_out, latents_out = pl.pallas_call(
        functools.partial(kernel, group),
        name="step",
        out_shape=(
            pltpu.VMEM((1, ROWS, part), BF16),
            pltpu.VMEM((PIECE, ROWS), F32),
        ),
        in_specs=[anywhere] * 18,
        out_specs=(vmem, vmem),
        scratch_shapes=[
            pltpu.SMEM((NX * NZ * NY,), jnp.int32),
            pltpu.SMEM((1, 1), jnp.int32),
            pltpu.SMEM((alphas.shape[0],), F32),
            pltpu.VMEM((1, PAIR), F32),
            pltpu.VMEM((HEAD,), F32),
            pltpu.VMEM((HEAD,), F32),
            pltpu.VMEM((ROWS, width), BF16),
            pltpu.VMEM((ROWS, width), BF16),
            pltpu.VMEM((ROWS, part), BF16),
            pltpu.VMEM((TXT, width), BF16),
            pltpu.VMEM((TXT, width), BF16),
            pltpu.VMEM((group, width, part), BF16),
            pltpu.VMEM((part,), F32),
            pltpu.VMEM((part,), F32),
            pltpu.VMEM((part,), F32),
            pltpu.VMEM((total * PIECE, part), F32),
            pltpu.VMEM((PIECE, ROWS), F32),
            pltpu.VMEM((width // PAIR, NZ, ROWS, PAIR), BF16),
            pltpu.VMEM((width // PAIR, n_kv, ROWS, PAIR), BF16),
            pltpu.VMEM((width // PAIR, n_kv, ROWS, PAIR), BF16),
            pltpu.VMEM((width // PAIR, NZ, ROWS, PAIR), BF16),
            pltpu.VMEM((width // PAIR, NZ, ROWS, PAIR), BF16),
            pltpu.VMEM((width // PAIR, NZ, 2, LANES), F32),
            pltpu.VMEM((width // PAIR, NZ, 2, LANES), F32),
            pltpu.VMEM((2, 16, LANES), F32),
            pltpu.VMEM((group, ROWS, part), F32),
            pltpu.VMEM((max(group - 1, 1), ROWS, part), BF16),
            pltpu.VMEM((group, ROWS, part), BF16),
            pltpu.VMEM((total, 8, LANES), F32),
            pltpu.VMEM((total, 8, LANES), F32),
            dma((18,)),
            dma((7,)),
            dma((18,)),
        ],
        compiler_params=pltpu.CompilerParams(collective_id=0, has_side_effects=True),
    )(
        lengths,
        step_index.reshape(1, 1),
        alphas,
        freq,
        q_gain,
        k_gain,
        stream,
        queries,
        keys,
        values,
        text_keys,
        text_values,
        out_weight,
        gate,
        shift,
        scale,
        proj_weight.T,
        latents.T,
    )
    return finish(hidden_out, latents_out)


def solution(mesh):
    return jax.shard_map(
        functools.partial(shards, mesh.shape["tp"]),
        mesh=mesh,
        in_specs=(
            P("cfg", "seq", "tp"),
            P("cfg", "seq", "tp"),
            P("cfg", "seq", "tp"),
            P("cfg", "seq", "tp"),
            P("cfg", None, "tp"),
            P("cfg", None, "tp"),
            P("tp", None),
            P("tp"),
            P("tp"),
            P("tp"),
            P("tp", None),
            P(),
            P(),
            P(),
            P("seq", ("cfg", "tp")),
            P(),
            P(),
        ),
        out_specs=(P("cfg", "seq", "tp"), P("seq", ("cfg", "tp"))),
        check_vma=False,
    )
```

```python
import functools

import jax
import jax.numpy as jnp
import numpy as np
from jax import lax
from jax.experimental import pallas as pl
from jax.experimental.pallas import tpu as pltpu
from jax.sharding import PartitionSpec as P

NX = 4
NZ = 8
NY = 2
D = 3072
HEAD = 64
HP = 30
WP = 45
STRIDE = 20
ROWS = 40
TXT = 226
LANES = 128
PAIR = 2 * HEAD
PIECE = 8
STATS = 16

guide_scale = 6.0
head_eps = 1e-06
final_eps = 1e-05
LOW = -1e30
NEAR, PART, LAST, QUERY, OTHER, FAR, STAT, OUT = 0, 1, 2, 3, 6, 9, 12, 15
MESH = pl.DeviceIdType.MESH
F32 = jnp.float32
BF16 = jnp.bfloat16


def frequencies():
    def one(extent):
        return 1.0 / 10000.0 ** (np.arange(0, extent, 2, dtype=np.float32) / np.float32(extent))

    freq = np.concatenate([one(16), one(24), one(24)]).astype(np.float32)
    return np.repeat(freq, 2)[None, :].repeat(2, axis=0).reshape(1, PAIR)


def nt(left, right, precision=None):
    return lax.dot_general(
        left, right, (((1,), (1,)), ((), ())), precision=precision, preferred_element_type=F32
    )


def nn(left, right, precision=None):
    return lax.dot_general(
        left, right, (((1,), (0,)), ((), ())), precision=precision, preferred_element_type=F32
    )


def kernel(
    group,
    lengths_hbm,
    step_index_hbm,
    alphas_hbm,
    freq_hbm,
    q_gain_hbm,
    k_gain_hbm,
    stream_hbm,
    queries_hbm,
    keys_hbm,
    values_hbm,
    text_keys_hbm,
    text_values_hbm,
    weight_hbm,
    gate_hbm,
    shift_hbm,
    scale_hbm,
    proj_hbm,
    latents_hbm,
    hidden_out,
    latents_out,
    lengths,
    step_index,
    alphas,
    freq,
    q_gain,
    k_gain,
    queries,
    keys,
    stream,
    text_keys,
    text_values,
    weight,
    gate,
    shift,
    scale,
    proj,
    latents,
    qbuf,
    kbuf,
    vbuf,
    osend,
    obuf,
    ssend,
    sbuf,
    sjoin,
    acc,
    rsend,
    rbuf,
    fsend,
    fbuf,
    load_sem,
    send_sem,
    recv_sem,
):
    n_kv = NX * NY
    total = 2 * group
    width = queries.shape[1]
    pairs = width // PAIR
    part = width * 2
    c = lax.axis_index("cfg")
    s = lax.axis_index("seq")
    t = lax.axis_index("tp")
    y = lax.rem(s, NY)
    z = lax.rem(lax.div(s, NY), NZ)
    x = lax.div(s, NY * NZ)
    rank = c * group + t

    def place(xx, zz, yy):
        return (c, (xx * NZ + zz) * NY + yy, t)

    z_of = [lax.rem(z + d, NZ) for d in range(1, NZ)]
    z_peers = [place(x, zz, y) for zz in z_of]
    x_of = [lax.rem(x + d, NX) for d in range(1, NX)]
    x_peers = [place(xx, z, y) for xx in x_of]
    y_peer = place(x, z, 1 - y)
    t_of = [t + 1 - 2 * lax.rem(t, 2), lax.rem(t + 2, group), group - 1 - t][: group - 1]
    t_peers = [(c, s, tt) for tt in t_of]
    g_of = [lax.rem(rank + d, total) for d in range(1, total)]
    g_peers = [(lax.div(g, group), s, lax.rem(g, group)) for g in g_of]

    barrier = pltpu.get_barrier_semaphore()
    everyone = z_peers + x_peers + ([y_peer] if NY > 1 else []) + g_peers
    for peer in everyone:
        pl.semaphore_signal(barrier, inc=1, device_id=peer, device_id_type=MESH)

    own = x * NY + y
    other = x * NY + (1 - y)

    def load(src, dst, which):
        copy = pltpu.make_async_copy(src, dst, load_sem.at[which])
        copy.start()
        return copy

    load_small = [
        load(lengths_hbm, lengths, 0),
        load(freq_hbm, freq, 1),
        load(q_gain_hbm, q_gain, 2),
        load(k_gain_hbm, k_gain, 3),
    ]
    load_k = load(keys_hbm.at[0], keys, 4)
    load_q = load(queries_hbm.at[0], queries, 5)
    for p in range(pairs):
        load(values_hbm.at[0, :, pl.ds(p * PAIR, PAIR)], vbuf.at[p, own], 6)
    load_text = [load(text_keys_hbm.at[0], text_keys, 7), load(text_values_hbm.at[0], text_values, 8)]
    for j in range(group):
        load(weight_hbm.at[:, pl.ds(j * part, part)], weight.at[j], 9)
    load_rest = [
        load(step_index_hbm, step_index, 10),
        load(alphas_hbm, alphas, 11),
        load(stream_hbm.at[0], stream, 12),
        load(gate_hbm, gate, 13),
        load(shift_hbm, shift, 14),
        load(scale_hbm, scale, 15),
        load(proj_hbm, proj, 16),
        load(latents_hbm, latents, 17),
    ]

    for copy in load_small:
        copy.wait()
    lane = lax.broadcasted_iota(jnp.int32, (1, PAIR), 1)
    within_head = lax.rem(lane, HEAD)
    is_even = lax.rem(lane, 2) == 0
    first_head = lane < HEAD
    own_start = jnp.int32(0)
    for b in range(NX * NZ * NY):
        own_start = own_start + jnp.where(b < s, lengths[b], 0)
    own_count = lengths[s]
    row = lax.broadcasted_iota(jnp.int32, (ROWS, PAIR), 0)
    live_rows = row < own_count
    position = (row + own_start).astype(F32)
    frame = jnp.floor((position + 0.5) * (1.0 / (HP * WP)))
    line = jnp.floor((position + 0.5) * (1.0 / WP))
    across = position - line * WP
    height = line - frame * HP
    coord = jnp.where(within_head < 16, frame, jnp.where(within_head < 40, height, across))
    angle = coord * freq[...]
    cos_table = jnp.cos(angle)
    sin_table = jnp.sin(angle)
    sin_table = jnp.where(is_even, -sin_table, sin_table)

    r_io = lax.broadcasted_iota(jnp.int32, (PAIR, PAIR), 0)
    c_io = lax.broadcasted_iota(jnp.int32, (PAIR, PAIR), 1)
    mean_matrix = jnp.where((r_io < HEAD) == (c_io < HEAD), 1.0 / HEAD, 0.0)
    mean_matrix_low = mean_matrix.astype(BF16)
    gain_q = q_gain[...].reshape(1, HEAD)
    gain_q = jnp.concatenate([gain_q, gain_q], axis=1)
    gain_k = k_gain[...].reshape(1, HEAD)
    gain_k = jnp.concatenate([gain_k, gain_k], axis=1)

    def head_norm(field, gain):
        centre = field.astype(F32) - nn(field, mean_matrix_low)
        square = centre * centre
        high = square.astype(BF16)
        low = (square - high.astype(F32)).astype(BF16)
        spread = nn(high, mean_matrix_low) + nn(low, mean_matrix_low)
        return centre * lax.rsqrt(spread + head_eps) * gain

    def rotate(field):
        swapped = jnp.where(
            is_even, pltpu.roll(field, PAIR - 1, 1), pltpu.roll(field, 1, 1)
        )
        return field * cos_table + swapped * sin_table

    def pair_slice(p):
        return pl.ds(p * PAIR, PAIR)

    load_k.wait()
    for p in range(pairs):
        made = rotate(head_norm(keys[:, pair_slice(p)], gain_k)).astype(BF16)
        kbuf[p, own] = made
    load_q.wait()
    for p in range(pairs):
        made = rotate(head_norm(queries[:, pair_slice(p)], gain_q)).astype(BF16)
        qbuf[p, z] = made
    pl.semaphore_wait(barrier, len(everyone))

    def send(src, dst, kind, which, peer):
        copy = pltpu.make_async_remote_copy(
            src_ref=src,
            dst_ref=dst,
            send_sem=send_sem.at[kind],
            recv_sem=recv_sem.at[which],
            device_id=peer,
            device_id_type=MESH,
        )
        copy.start()

    def whole_copy(ref, kind, which):
        return pltpu.make_async_remote_copy(
            src_ref=ref,
            dst_ref=ref,
            send_sem=send_sem.at[kind],
            recv_sem=recv_sem.at[which],
            device_id=g_peers[0],
            device_id_type=MESH,
        )

    def arrive(ref, which):
        whole_copy(ref, 0, which).wait_recv()

    for p in range(pairs):
        if NY > 1:
            for to in (y_peer,):
                send(kbuf.at[p, own], kbuf.at[p, own], 0, OTHER + p, to)
                send(values_hbm.at[0, :, pair_slice(p)], vbuf.at[p, own], 1, OTHER + p, to)
    for p in range(pairs):
        for to in x_peers:
            send(kbuf.at[p, own], kbuf.at[p, own], 0, NEAR, to)
            send(values_hbm.at[0, :, pair_slice(p)], vbuf.at[p, own], 1, NEAR, to)

    order_z = sorted(range(1, NZ), key=lambda d: -min(d, NZ - d))
    for p in range(pairs):
        for d in order_z:
            send(qbuf.at[p, z], qbuf.at[p, z], 2, QUERY + p, z_peers[d - 1])

    for copy in load_text:
        copy.wait()
    text_mixed = []
    lane_row = lax.broadcasted_iota(jnp.int32, (ROWS, LANES), 1)
    text_stat = jnp.where(lax.rem(lane_row, 8) >= 6, 1.0, 0.0)
    for p in range(pairs):
        made = head_norm(text_keys[:, pair_slice(p)], gain_k)
        query_part = qbuf[p, z]
        value_part = text_values[:, pair_slice(p)]
        outs = []
        for which in range(2):
            chosen = first_head if which == 0 else jnp.logical_not(first_head)
            key_part = jnp.where(chosen, made, 0.0).astype(BF16)
            scores = nt(query_part, key_part) * 0.125
            top = jnp.max(scores, axis=1, keepdims=True)
            weights = jnp.exp(scores - top)
            count = jnp.sum(weights, axis=1, keepdims=True)
            outs.append(nn(weights.astype(BF16), value_part))
            head = 2 * p + which
            text_stat = jnp.where(lane_row == head, top, text_stat)
            text_stat = jnp.where(lane_row == 8 + head, count, text_stat)
        text_mixed.append(jnp.where(first_head, outs[0], outs[1]))
    below = jnp.zeros((LANES - ROWS, LANES), F32)
    text_stat = jnp.concatenate([text_stat, below], axis=0).T
    lane_tile = lax.broadcasted_iota(jnp.int32, (8, LANES), 1)
    text_stat = jnp.where(
        lane_tile < HEAD, text_stat[0:8], pltpu.roll(text_stat[8:16], HEAD, 1)
    )

    for p in range(pairs):
        if NY > 1:
            arrive(kbuf.at[p, pl.ds(0, 2)], OTHER + p)
            for to in x_peers:
                send(kbuf.at[p, other], kbuf.at[p, other], 0, FAR + p, to)
                send(vbuf.at[p, other], vbuf.at[p, other], 1, FAR + p, to)
    arrive(kbuf.at[:, pl.ds(0, 2 * (NX - 1))], NEAR)
    pltpu.make_async_copy(vbuf.at[:, 0], vbuf.at[:, 0], load_sem.at[6]).wait()

    n_keys = NX * ROWS
    n_queries = NZ * ROWS
    q_up = -(-n_queries // LANES) * LANES
    slot_row = lax.broadcasted_iota(jnp.int32, (ROWS, 1), 0)

    def gather(buf, p, yy):
        blocks = [buf[p, j * NY + yy].astype(F32) for j in range(NX)]
        return jnp.concatenate(blocks, axis=0)

    def live_of(yy):
        pieces = [
            jnp.where(slot_row < lengths[(j * NZ + z) * NY + yy], 0.0, LOW) for j in range(NX)
        ]
        return jnp.concatenate(pieces + pieces, axis=0)

    def score(p, yy, live):
        key_part = gather(kbuf, p, yy)
        both = jnp.concatenate(
            [jnp.where(first_head, key_part, 0.0), jnp.where(first_head, 0.0, key_part)], axis=0
        ).astype(BF16)
        found = jnp.where(live < 0.0, LOW, nt(both, query_parts[p]) * 0.125)
        turned = gather(vbuf, p, yy).T.astype(BF16)
        return [
            (found[w * n_keys : (w + 1) * n_keys], turned[w * HEAD : (w + 1) * HEAD])
            for w in range(2)
        ]

    query_parts = []
    partials = []
    live_near = live_of(y)
    live_far = live_of(1 - y)
    stat_row = lax.broadcasted_iota(jnp.int32, (8, q_up), 0)

    def widen(line):
        if q_up == n_queries:
            return line
        return jnp.concatenate([line, jnp.zeros((line.shape[0], q_up - n_queries), F32)], axis=1)

    def near(p):
        arrive(qbuf.at[p, pl.ds(0, NZ - 1)], QUERY + p)
        query_parts.append(
            jnp.concatenate([qbuf[p, j].astype(F32) for j in range(NZ)], axis=0).astype(BF16)
        )
        for scores, turned in score(p, y, live_near):
            top = jnp.max(scores, axis=0, keepdims=True)
            weights = jnp.exp(scores - top)
            count = jnp.sum(weights, axis=0, keepdims=True)
            partials.append((top, count, nn(turned, weights.astype(BF16))))

    def far(p):
        outs, tops, counts = [], None, None
        if NY > 1:
            arrive(kbuf.at[p, pl.ds(0, 2 * (NX - 1))], FAR + p)
            scored = score(p, 1 - y, live_far)
        for which in range(2):
            top, count, out = partials[2 * p + which]
            if NY > 1:
                scores, turned = scored[which]
                before = top
                top = jnp.maximum(before, jnp.max(scores, axis=0, keepdims=True))
                fade = jnp.exp(before - top)
                weights = jnp.exp(scores - top)
                count = count * fade + jnp.sum(weights, axis=0, keepdims=True)
                out = out * fade + nn(turned, weights.astype(BF16))
            outs.append(out)
            tops = widen(top) if which == 0 else jnp.where(stat_row == 0, tops, widen(top))
            counts = widen(count) if which == 0 else jnp.where(stat_row == 0, counts, widen(count))
        mixed = widen(jnp.concatenate(outs, axis=0)).T
        for j in range(NZ):
            osend[p, j] = mixed[j * ROWS : (j + 1) * ROWS].astype(BF16)
        for d in order_z:
            zz = z_of[d - 1]
            send(osend.at[p, zz], obuf.at[p, z], 4, OUT + p, z_peers[d - 1])
        for j in range(NZ):
            left = pltpu.roll(tops, (q_up - j * ROWS) % q_up, 1)[:, 0:LANES]
            right = pltpu.roll(counts, (q_up + HEAD - j * ROWS) % q_up, 1)[:, 0:LANES]
            ssend[p, j] = jnp.where(lane_tile < HEAD, left, right)[0:2]
        for d in order_z:
            zz = z_of[d - 1]
            send(ssend.at[p, zz], sbuf.at[p, z], 3, STAT + p, z_peers[d - 1])

    near(0)
    for p in range(1, pairs):
        near(p)
        far(p - 1)
    far(pairs - 1)

    pltpu.make_async_copy(weight, weight, load_sem.at[9]).wait()
    for w in range(2):
        sjoin[w] = jnp.where(lax.broadcasted_iota(jnp.int32, (16, LANES), 1) < HEAD, LOW, 0.0)
    for p in range(pairs):
        arrive(sbuf.at[p, pl.ds(0, NZ - 1)], STAT + p)
        arrive(obuf.at[p, pl.ds(0, NZ - 1)], OUT + p)
        stats = [ssend[p, z]] + [sbuf[p, zz] for zz in z_of] + [text_stat[2 * p : 2 * p + 2]]
        for w in range(2):
            for j, one in enumerate(stats):
                sjoin[w, j : j + 1, :] = one[w : w + 1]
        shares = []
        for w in range(2):
            found = sjoin[w]
            count = pltpu.roll(found, HEAD, 1)
            factor = jnp.exp(found - jnp.max(found, axis=0, keepdims=True))
            shares.append(factor / jnp.sum(factor * count, axis=0, keepdims=True))
        share = jnp.concatenate(shares + [jnp.zeros((LANES - 32, LANES), F32)], axis=0).T
        pieces = [osend[p, z]] + [obuf[p, zz] for zz in z_of]
        pieces = [piece.astype(F32) for piece in pieces] + [text_mixed[p]]
        joined = jnp.zeros((ROWS, PAIR), F32)
        for j, piece in enumerate(pieces):
            lower = share[0:ROWS, j : j + 1]
            upper = share[0:ROWS, 16 + j : 17 + j]
            joined = joined + piece * jnp.where(first_head, lower, upper)
        attended = joined.astype(BF16)
        if p < pairs - 1:
            for j in range(group):
                more = nn(attended, weight[j, pair_slice(p), :])
                acc[j] = more if p == 0 else acc[j] + more
    for d in range(1, group):
        tt = t_of[d - 1]
        rsend[d - 1] = (acc[tt] + nn(attended, weight[tt, pair_slice(pairs - 1), :])).astype(BF16)
        send(rsend.at[d - 1], rbuf.at[t], 5, PART, t_peers[d - 1])
    summed = acc[t] + nn(attended, weight[t, pair_slice(pairs - 1), :])
    for copy in load_rest:
        copy.wait()
    lifted = 1.0 + scale[...].reshape(1, part)
    arrive(rbuf.at[pl.ds(0, group - 1)], PART)
    for tt in t_of:
        summed = summed + rbuf[tt].astype(F32)
    hidden = stream[...].astype(F32) + gate[...].reshape(1, part) * summed
    hidden = jnp.where(live_rows[:, 0:1], hidden, 0.0).astype(BF16)
    hidden_out[0] = hidden
    widened = hidden.astype(F32)

    channels = total * PIECE
    tall = ROWS + 8
    extra = jnp.concatenate([lifted, shift[...].reshape(1, part), jnp.zeros((6, part), F32)], axis=0)
    stacked = jnp.concatenate([widened * lifted, extra], axis=0)
    flipped = nt(proj[...], stacked, lax.Precision.HIGHEST)
    row_sum = nt(jnp.ones((8, part), BF16), hidden)
    row_square = nt(jnp.ones((8, part), F32), widened * widened, lax.Precision.HIGHEST)
    flipped = jnp.concatenate([flipped, jnp.zeros((channels, HEAD - tall), F32)], axis=1)
    sums = jnp.where(lax.broadcasted_iota(jnp.int32, (8, ROWS), 0) == 0, row_sum, row_square)
    sums = jnp.concatenate([sums, jnp.zeros((8, HEAD - ROWS), F32)], axis=1)
    for g in range(total):
        fsend[g] = jnp.concatenate([flipped[g * PIECE : (g + 1) * PIECE], sums], axis=1)
    for d in range(1, total):
        g = g_of[d - 1]
        send(fsend.at[g], fbuf.at[rank], 6, LAST, g_peers[d - 1])
    arrive(fbuf.at[pl.ds(0, total - 1)], LAST)

    def prediction(half):
        gathered = jnp.zeros((8, LANES), F32)
        for tt in range(group):
            g = half * group + tt
            gathered = gathered + jnp.where(rank == g, fsend[g], fbuf[g])
        sums = pltpu.roll(gathered, HEAD, 1)
        mean = sums[0:1] / D
        square = sums[1:2] / D
        base = gathered
        ratio = lax.rsqrt(square - mean * mean + final_eps)
        lifted_sum = base[:, ROWS : ROWS + 1]
        shift_sum = base[:, ROWS + 1 : ROWS + 2]
        return ratio * (base - mean * lifted_sum) + shift_sum

    conditioned = prediction(0)
    unconditioned = prediction(1)
    guided = unconditioned + guide_scale * (conditioned - unconditioned)
    guided = guided[:, 0:ROWS]
    step = step_index[0, 0]
    current = jnp.zeros((1, ROWS), F32) + alphas[step]
    earlier = jnp.zeros((1, ROWS), F32) + alphas[jnp.maximum(step - STRIDE, 0)]
    root_now = jnp.sqrt(current)
    rest_now = jnp.sqrt(1.0 - current)
    held = latents[...]
    clean = root_now * held - rest_now * guided
    noise = root_now * guided + rest_now * held
    stepped = jnp.sqrt(earlier) * clean + jnp.sqrt(1.0 - earlier) * noise
    token = lax.broadcasted_iota(jnp.int32, (1, ROWS), 1)
    latents_out[...] = jnp.where(token < own_count, stepped, 0.0)

    n_block = NX - 1 + (NX if NY > 1 else 0)
    for kind, ref in enumerate(
        [
            kbuf.at[:, pl.ds(0, n_block)],
            vbuf.at[:, pl.ds(0, n_block)],
            qbuf.at[:, pl.ds(0, NZ - 1)],
            sbuf.at[:, pl.ds(0, NZ - 1)],
            obuf.at[:, pl.ds(0, NZ - 1)],
            rbuf.at[pl.ds(0, group - 1)],
            fbuf.at[pl.ds(0, total - 1)],
        ]
    ):
        whole_copy(ref, kind, 0).wait_send()


def finish_kernel(hidden, latents, hidden_out, latents_out, sem):
    copies = [
        pltpu.make_async_copy(hidden, hidden_out, sem.at[0]),
        pltpu.make_async_copy(latents, latents_out, sem.at[1]),
    ]
    for copy in copies:
        copy.start()
    for copy in copies:
        copy.wait()


def finish(hidden, latents):
    vmem = pl.BlockSpec(memory_space=pltpu.VMEM)
    anywhere = pl.BlockSpec(memory_space=pl.ANY)
    hidden, latents = pl.pallas_call(
        finish_kernel,
        name="finish",
        out_shape=(
            jax.ShapeDtypeStruct(hidden.shape, hidden.dtype),
            jax.ShapeDtypeStruct(latents.shape, latents.dtype),
        ),
        in_specs=[vmem, vmem],
        out_specs=(anywhere, anywhere),
        scratch_shapes=[pltpu.SemaphoreType.DMA((2,))],
    )(
        pltpu.with_memory_space_constraint(hidden, pltpu.VMEM),
        pltpu.with_memory_space_constraint(latents, pltpu.VMEM),
    )
    return hidden, latents.T


def shards(
    group,
    stream,
    queries,
    keys,
    values,
    text_keys,
    text_values,
    out_weight,
    gate,
    shift,
    scale,
    proj_weight,
    q_gain,
    k_gain,
    lengths,
    latents,
    alphas,
    step_index,
):
    width = queries.shape[2]
    part = stream.shape[2]
    n_kv = NX * NY
    total = 2 * group
    freq = jnp.asarray(frequencies())
    vmem = pl.BlockSpec(memory_space=pltpu.VMEM)
    anywhere = pl.BlockSpec(memory_space=pl.ANY)
    dma = pltpu.SemaphoreType.DMA
    hidden_out, latents_out = pl.pallas_call(
        functools.partial(kernel, group),
        name="step",
        out_shape=(
            pltpu.VMEM((1, ROWS, part), BF16),
            pltpu.VMEM((PIECE, ROWS), F32),
        ),
        in_specs=[anywhere] * 18,
        out_specs=(vmem, vmem),
        scratch_shapes=[
            pltpu.SMEM((NX * NZ * NY,), jnp.int32),
            pltpu.SMEM((1, 1), jnp.int32),
            pltpu.SMEM((alphas.shape[0],), F32),
            pltpu.VMEM((1, PAIR), F32),
            pltpu.VMEM((HEAD,), F32),
            pltpu.VMEM((HEAD,), F32),
            pltpu.VMEM((ROWS, width), BF16),
            pltpu.VMEM((ROWS, width), BF16),
            pltpu.VMEM((ROWS, part), BF16),
            pltpu.VMEM((TXT, width), BF16),
            pltpu.VMEM((TXT, width), BF16),
            pltpu.VMEM((group, width, part), BF16),
            pltpu.VMEM((part,), F32),
            pltpu.VMEM((part,), F32),
            pltpu.VMEM((part,), F32),
            pltpu.VMEM((total * PIECE, part), F32),
            pltpu.VMEM((PIECE, ROWS), F32),
            pltpu.VMEM((width // PAIR, NZ, ROWS, PAIR), BF16),
            pltpu.VMEM((width // PAIR, n_kv, ROWS, PAIR), BF16),
            pltpu.VMEM((width // PAIR, n_kv, ROWS, PAIR), BF16),
            pltpu.VMEM((width // PAIR, NZ, ROWS, PAIR), BF16),
            pltpu.VMEM((width // PAIR, NZ, ROWS, PAIR), BF16),
            pltpu.VMEM((width // PAIR, NZ, 2, LANES), F32),
            pltpu.VMEM((width // PAIR, NZ, 2, LANES), F32),
            pltpu.VMEM((2, 16, LANES), F32),
            pltpu.VMEM((group, ROWS, part), F32),
            pltpu.VMEM((max(group - 1, 1), ROWS, part), BF16),
            pltpu.VMEM((group, ROWS, part), BF16),
            pltpu.VMEM((total, 8, LANES), F32),
            pltpu.VMEM((total, 8, LANES), F32),
            dma((18,)),
            dma((7,)),
            dma((18,)),
        ],
        compiler_params=pltpu.CompilerParams(collective_id=0, has_side_effects=True),
    )(
        lengths,
        step_index.reshape(1, 1),
        alphas,
        freq,
        q_gain,
        k_gain,
        stream,
        queries,
        keys,
        values,
        text_keys,
        text_values,
        out_weight,
        gate,
        shift,
        scale,
        proj_weight.T,
        latents.T,
    )
    return finish(hidden_out, latents_out)


def solution(mesh):
    return jax.shard_map(
        functools.partial(shards, mesh.shape["tp"]),
        mesh=mesh,
        in_specs=(
            P("cfg", "seq", "tp"),
            P("cfg", "seq", "tp"),
            P("cfg", "seq", "tp"),
            P("cfg", "seq", "tp"),
            P("cfg", None, "tp"),
            P("cfg", None, "tp"),
            P("tp", None),
            P("tp"),
            P("tp"),
            P("tp"),
            P("tp", None),
            P(),
            P(),
            P(),
            P("seq", ("cfg", "tp")),
            P(),
            P(),
        ),
        out_specs=(P("cfg", "seq", "tp"), P("seq", ("cfg", "tp"))),
        check_vma=False,
    )
```
